512 devices in a mesh: ctx: 64 (over x, z_lo, y), head: 8 (over z_hi, core).
Axes of the slice: x: 4, y: 8, z: 8 (z_hi: 4, z_lo: 2; z = z_hi * 2 + z_lo), core: 2. Of those that a mesh axis runs over, the one named last changes fastest.
Arguments:
- queries: bfloat16 [16384, 4096], P('ctx', 'head'), may hold values from -12 to 12
- keys: bfloat16 [16384, 4096], P('ctx', 'head'), may hold values from -4 to 4
- values: bfloat16 [16384, 4096], P('ctx', 'head'), may hold values from -6 to 6
- pool_weight: bfloat16 [512, 256], P('ctx'), may hold values from -0.375 to 0.375
- out_weight: bfloat16 [4096, 4096], P('head', 'ctx'), may hold values from -0.09375 to 0.09375
- pattern: int32 [128, 7], replicated, may hold values from 0 to 127, as said below
Outputs:
- mixed: bfloat16 [16384, 4096], P('ctx', 'head')
The draws below stay inside these ranges and needn't reach their ends.
Inputs may be any that keep to these rules, and one draw needn't show every extreme that they name: `pattern`: the flat butterfly with the blocks of each shard relabelled: entry (i, b) names a key block that agrees with block i in all bits above b and differs from it in bit b. For b < 1 the lower bits are arbitrary. For b >= 1 the bits from 1 to b - 1 equal those of i, and over the 2 query blocks of one aligned group of 2 blocks the lowest 1 bits take each of their 2 values once.
All inputs are finite; a program needn't handle non-finite values.
Results may differ from the reference program's by a relative error of at most 0.019.
Values may be sent and summed in bfloat16 or wider, within the bound.
No kernel may reach another device: no remote copies, remote signals or barrier semaphores. Data moves between devices by JAX's collectives and lax.ppermute only.
A program may use at most 64 MiB of HBM per device.

```python
import jax
import jax.numpy as jnp
from jax import lax

D = 4096
ATTENTION_HEADS = 32
HEAD_DIMENSION = 128
BLK = 128
LAND = 8
TOK_DEV = 256
BPS = 2
LOCAL_BITS = 1
NBITS = 7
TOKENS = 16384
NBLK = 128
LANDMARK_TOTAL = 512
N_CTX = 64
N_HEAD = 8


def draw_queries(key, part):
    drawn_part = jnp.clip(2.5 * jax.random.normal(jax.random.fold_in(key, 1), (TOKENS, ATTENTION_HEADS * HEAD_DIMENSION)), -12.0, 12.0)
    return drawn_part.astype(jnp.bfloat16)


def draw_keys(key, part):
    drawn_part = jnp.clip(jax.random.normal(jax.random.fold_in(key, 2), (TOKENS, ATTENTION_HEADS * HEAD_DIMENSION)), -4.0, 4.0)
    return drawn_part.astype(jnp.bfloat16)


def draw_pattern(key, part):
    block_index = jnp.arange(NBLK, dtype=jnp.int32)
    group_count = NBLK // BPS
    columns = []
    for level in range(NBITS):
        upper = block_index >> level + 1 << level + 1
        flipped = (block_index >> level & 1 ^ 1) << level
        if level < LOCAL_BITS:
            if level > 0:
                lower = jax.random.randint(jax.random.fold_in(key, level), (NBLK,), 0, 2 ** level).astype(jnp.int32)
            else:
                lower = jnp.zeros((NBLK,), jnp.int32)
            columns.append(upper | flipped | lower)
        else:
            middle = block_index & (1 << level) - BPS
            group_keys = jax.random.split(jax.random.fold_in(key, 100 + level), group_count)
            leaf = jax.vmap(lambda sub_key: jax.random.permutation(sub_key, BPS))(group_keys).reshape(NBLK).astype(jnp.int32)
            columns.append(upper | flipped | middle | leaf)
    return jnp.stack(columns, axis=1).astype(jnp.int32)


def level_of(key, shape, cuts, smallest, top_value):
    loudness = 1.0
    for position, blocks in cuts:
        steps = jax.random.uniform(jax.random.fold_in(jax.random.fold_in(key, 6), position), (blocks,), jnp.float32, smallest / len(cuts), top_value / len(cuts))
        loudness = loudness * jnp.repeat(jnp.exp(steps), shape[position] // blocks).reshape((-1,) + (1,) * (len(shape) - 1 - position))
    return loudness


def scatter_about(stream_key, extent, spread, limit, cuts=(), kind=jnp.bfloat16):
    factor_of = level_of(stream_key, extent, cuts, -0.22, 0.18) if cuts else 1.0
    drawn = jax.random.normal(stream_key, extent, jnp.float32) * spread * factor_of
    return jnp.minimum(jnp.maximum(drawn, -limit), limit).astype(kind)


def setup_inputs(seed: int = 0) -> dict:
    seeds = jax.random.split(jax.random.key(seed), 7)
    return {
        "queries": draw_queries(jax.random.fold_in(seeds[6], 71), 0),
        "keys": draw_keys(jax.random.fold_in(seeds[6], 71), 0),
        "values": scatter_about(seeds[2], (TOKENS, ATTENTION_HEADS * HEAD_DIMENSION), 1.0, 6.0, ((0, 64), (1, 8))),
        "pool_weight": scatter_about(seeds[3], (LANDMARK_TOTAL, TOK_DEV), TOK_DEV ** -0.5, 0.375, ((0, 64),)),
        "out_weight": scatter_about(seeds[4], (ATTENTION_HEADS * HEAD_DIMENSION, D), (ATTENTION_HEADS * HEAD_DIMENSION) ** -0.5, 0.09375, ((0, 8), (1, 64))),
        "pattern": draw_pattern(jax.random.fold_in(seeds[6], 71), 0),
    }


def reference(queries, keys, values, pool_weight, out_weight, pattern):
    col_width = ATTENTION_HEADS * HEAD_DIMENSION
    sharded_keys = keys.reshape(N_CTX, TOK_DEV, col_width).astype(jnp.float32)
    sharded_values = values.reshape(N_CTX, TOK_DEV, col_width).astype(jnp.float32)
    sharded_pooling = pool_weight.reshape(N_CTX, LAND, TOK_DEV).astype(jnp.float32)
    pooled_landmark_keys = jnp.einsum("rmi,riu->rmu", sharded_pooling, sharded_keys).astype(jnp.bfloat16).reshape(LANDMARK_TOTAL, ATTENTION_HEADS, HEAD_DIMENSION)
    pooled_landmark_values = jnp.einsum("rmi,riu->rmu", sharded_pooling, sharded_values).astype(jnp.bfloat16).reshape(LANDMARK_TOTAL, ATTENTION_HEADS, HEAD_DIMENSION)
    key_blocks = keys.reshape(NBLK, BLK, ATTENTION_HEADS, HEAD_DIMENSION)
    value_blocks = values.reshape(NBLK, BLK, ATTENTION_HEADS, HEAD_DIMENSION)
    query_blocks = queries.reshape(NBLK, BLK, ATTENTION_HEADS, HEAD_DIMENSION)
    score_scale = HEAD_DIMENSION ** -0.5

    def one_block(block_index):
        chosen = jnp.concatenate([jnp.reshape(block_index, (1,)).astype(jnp.int32), pattern[block_index].astype(jnp.int32)])
        key_set = jnp.concatenate([key_blocks[chosen].reshape(-1, ATTENTION_HEADS, HEAD_DIMENSION), pooled_landmark_keys], axis=0)
        value_set = jnp.concatenate([value_blocks[chosen].reshape(-1, ATTENTION_HEADS, HEAD_DIMENSION), pooled_landmark_values], axis=0)
        scores = jnp.einsum("qhd,khd->hqk", query_blocks[block_index].astype(jnp.float32), key_set.astype(jnp.float32)) * score_scale
        row_max = jnp.max(scores, axis=-1, keepdims=True)
        weights = jnp.exp(scores - row_max)
        row_sum = jnp.sum(weights, axis=-1)
        rounded = lax.optimization_barrier(weights.astype(jnp.bfloat16))
        summed = jnp.einsum("hqk,khd->qhd", rounded.astype(jnp.float32), value_set.astype(jnp.float32))
        return (summed / row_sum.T[:, :, None]).astype(jnp.bfloat16)

    attended = lax.map(one_block, jnp.arange(NBLK, dtype=jnp.int32))
    group_width = col_width // N_HEAD
    attended = attended.reshape(N_CTX, TOK_DEV, N_HEAD, group_width)
    weight_groups = out_weight.reshape(N_HEAD, group_width, D).astype(jnp.float32)

    def project(shard_rows):
        parts = jnp.einsum("tgc,gcd->gtd", shard_rows.astype(jnp.float32), weight_groups).astype(jnp.bfloat16)
        parts = lax.optimization_barrier(parts)
        return jnp.sum(parts.astype(jnp.float32), axis=0).astype(jnp.bfloat16)

    mixed = lax.map(project, attended)
    return mixed.reshape(TOKENS, D)
```

```python
import functools

import jax
import jax.numpy as jnp
from jax import lax
from jax.experimental import pallas as pl
from jax.experimental.pallas import tpu as pltpu
from jax.sharding import PartitionSpec as P

HD = 128
BLK = 128
NX, NZL, NY, NZH, NC = 4, 2, 8, 4, 2
WROWS = 64
LROWS = 16
UNIT = WROWS + LROWS
AXES = ("ctx", "head")
SCALE = HD**-0.5
F32 = jnp.float32
BF16 = jnp.bfloat16
VLIM = 16 << 20


def coords(i):
    ctx, head = divmod(i, NZH * NC)
    x, r = divmod(ctx, NZL * NY)
    zl, y = divmod(r, NY)
    zh, c = divmod(head, NC)
    return x, zl, y, zh, c


def flat(x, zl, y, zh, c):
    return ((x * NZL + zl) * NY + y) * (NZH * NC) + zh * NC + c


def send(a, to):
    pairs = [(i, flat(*to(*coords(i)))) for i in range(NX * NZL * NY * NZH * NC)]
    return lax.ppermute(a, AXES, pairs)


def along_x(k):
    return lambda x, zl, y, zh, c: ((x + k) % NX, zl, y, zh, c)


def xor(level):
    def to(x, zl, y, zh, c):
        ctx = ((x * NZL + zl) * NY + y) ^ (1 << level)
        x, r = divmod(ctx, NZL * NY)
        zl, y = divmod(r, NY)
        return x, zl, y, zh, c

    return to


def after(a, far, levels):
    if levels:
        a, done = lax.optimization_barrier((a, [far[l] for l in levels]))
        far.update(zip(levels, done, strict=True))
    return a


def vmem(n):
    return [pl.BlockSpec(memory_space=pltpu.VMEM)] * n


SMEM = pl.BlockSpec(memory_space=pltpu.SMEM)


def params():
    return pltpu.CompilerParams(vmem_limit_bytes=VLIM)


def dot_nt(a, b):
    return lax.dot_general(a, b, (((1,), (1,)), ((), ())), preferred_element_type=F32)


def prepare_kernel(pool, keys, values, weight, kv, unit):
    k, v = keys[...], values[...]
    kv[0:256, :] = k
    kv[256:512, :] = v
    unit[0:WROWS, :] = weight[...].astype(F32).T.astype(BF16)
    pooled = [jnp.dot(pool[...], a, preferred_element_type=F32) for a in (k, v)]
    unit[WROWS:UNIT, :] = jnp.concatenate(pooled, axis=0).astype(BF16)


def prepare(pool, keys, values, weight):
    return pl.pallas_call(
        prepare_kernel,
        out_shape=(
            jax.ShapeDtypeStruct((512, 512), BF16),
            jax.ShapeDtypeStruct((UNIT, 512), BF16),
        ),
        in_specs=vmem(4),
        out_specs=tuple(vmem(2)),
        compiler_params=params(),
        name="prepare",
    )(pool, keys, values, weight)


def softmax_step(state, q, ks, vs):
    scores = [dot_nt(q, k) * SCALE for k in ks]
    top = functools.reduce(jnp.maximum, [jnp.max(s, axis=1, keepdims=True) for s in scores])
    if state is not None:
        old_top, old_sum, old_acc = state
        top = jnp.maximum(top, old_top)
    weights = [jnp.exp(s - top) for s in scores]
    total = sum(jnp.sum(w, axis=1, keepdims=True) for w in weights)
    acc = sum(
        jnp.dot(w.astype(BF16), v, preferred_element_type=F32)
        for w, v in zip(weights, vs, strict=True)
    )
    if state is not None:
        fade = jnp.exp(old_top - top)
        total = total + old_sum * fade
        acc = acc + old_acc * fade
    return top, total, acc


def far_blocks(place, pattern, j, level, ref):
    at = pl.multiple_of((pattern[place[3] + j, 1 + level] & 1) * BLK, BLK)
    return ref[pl.ds(at, BLK), :], ref[pl.ds(256 + at, BLK), :]


def by_head(rows):
    return pl.BlockSpec((rows, HD), lambda h: (0, h))


def first_kernel(levels, place, pattern, q, own, *refs):
    far, (top, total, acc) = refs[:-3], refs[-3:]
    for j in range(2):
        rows = slice(j * BLK, (j + 1) * BLK)
        ks, vs = [own[0:256, :]], [own[256:512, :]]
        for level, ref in zip(levels, far, strict=True):
            k, v = far_blocks(place, pattern, j, level, ref)
            ks.append(k)
            vs.append(v)
        m, s, a = softmax_step(None, q[rows, :], ks, vs)
        top[rows, :] = jnp.broadcast_to(m, (BLK, HD))
        total[rows, :] = jnp.broadcast_to(s, (BLK, HD))
        acc[rows, :] = a


def first(levels, place, pattern, q, own, far):
    return pl.pallas_call(
        functools.partial(first_kernel, levels),
        grid=(4,),
        out_shape=(jax.ShapeDtypeStruct((256, 512), F32),) * 3,
        in_specs=[SMEM, SMEM, by_head(256)] + [by_head(512)] * (1 + len(far)),
        out_specs=(by_head(256),) * 3,
        compiler_params=params(),
        name="first",
        cost_estimate=pl.CostEstimate(
            flops=4 * 256 * 512 * 768, bytes_accessed=4 << 20, transcendentals=786432
        ),
    )(place, pattern, q, own, *far)


def landmarks(units):
    ks, vs = [], []
    for ref, starts in units:
        for at in starts:
            pair = ref[at : at + LROWS, :].astype(F32)
            ks.append(pair[0:8])
            vs.append(pair[8:16])
    return jnp.concatenate(ks, axis=0).astype(BF16), jnp.concatenate(vs, axis=0).astype(BF16)


def lm_starts(lo, hi):
    rows = [b * UNIT + WROWS for b in range(NY)] + [NY * UNIT + b * LROWS for b in range(NY)]
    return [r - lo for r in rows if lo <= r < hi]


def last_kernel(levels, place, pattern, q, top, total, acc, wl0, wl1, wl3, wl2a, wl2b, *refs):
    far, out = refs[:-1], refs[-1]
    units = [(r, lm_starts(0, 768)) for r in (wl0, wl1, wl3)]
    units += [(wl2a, lm_starts(0, 400)), (wl2b, lm_starts(400, 768))]
    mark_k, mark_v = landmarks(units)
    for j in range(2):
        rows = slice(j * BLK, (j + 1) * BLK)
        ks, vs = [mark_k], [mark_v]
        for level, ref in zip(levels, far, strict=True):
            k, v = far_blocks(place, pattern, j, level, ref)
            ks.append(k)
            vs.append(v)
        state = (top[rows, 0:1], total[rows, 0:1], acc[rows, :])
        _, s, a = softmax_step(state, q[rows, :], ks, vs)
        out[rows, :] = (a / s).astype(BF16)


def last(levels, place, pattern, q, state, wl, far):
    return pl.pallas_call(
        functools.partial(last_kernel, levels),
        grid=(4,),
        out_shape=jax.ShapeDtypeStruct((256, 512), BF16),
        in_specs=[SMEM, SMEM]
        + [by_head(256)] * 4
        + [by_head(a.shape[0]) for a in wl]
        + [by_head(512)] * len(far),
        out_specs=by_head(256),
        compiler_params=params(),
        name="last",
        cost_estimate=pl.CostEstimate(
            flops=4 * 256 * 512 * 768, bytes_accessed=8 << 20, transcendentals=786432
        ),
    )(place, pattern, q, *state, *wl, *far)


def w_rows(pieces):
    out = []
    for y in range(NY):
        at = ((y & 1) * 4 + (y & 2) + (y >> 2)) * UNIT
        for ref, lo, hi in pieces:
            a, b = max(at, lo), min(at + WROWS, hi)
            if a < b:
                out.append(ref[a - lo : b - lo, :])
    return jnp.concatenate(out, axis=0)


def project_kernel(place, mine, other, wl0, wl1, wl3, wl2a, wl2b, keep, give):
    x, zh, same = place[0], place[1], place[2]
    swap = same == 0
    a, b = mine[...], other[...]
    kept = jnp.where(swap, b, a)
    given = jnp.where(swap, a, b)
    chunks = [(0, [(wl0, 0, 768)]), (1, [(wl1, 0, 768)]), (3, [(wl3, 0, 768)])]
    chunks += [(2, [(wl2a, 0, 400), (wl2b, 400, 768)])]
    for shift, pieces in chunks:
        w = w_rows(pieces)
        d = lax.rem(x + 8 - shift - zh, 4)
        give[d] = dot_nt(given, w).astype(BF16)
        keep[d] = dot_nt(kept, w)


def project(place, mine, other, wl):
    return pl.pallas_call(
        project_kernel,
        out_shape=(
            jax.ShapeDtypeStruct((4, 256, 512), F32),
            jax.ShapeDtypeStruct((4, 256, 512), BF16),
        ),
        in_specs=[SMEM, *vmem(7)],
        out_specs=tuple(vmem(2)),
        compiler_params=params(),
        name="project",
        cost_estimate=pl.CostEstimate(
            flops=2 * 512 * 512 * 2048, bytes_accessed=6 << 20, transcendentals=0
        ),
    )(place, mine, other, *wl)


def on_device(queries, keys, values, pool_weight, out_weight, pattern):
    ctx, head = lax.axis_index("ctx"), lax.axis_index("head")
    x, zl, y = ctx // (NZL * NY), (ctx // NY) % NZL, ctx % NY
    zh, c = head // NC, head % NC
    place = jnp.stack([x, zh, (zl == c).astype(jnp.int32), ctx * 2])

    kv, unit = prepare(pool_weight, keys, values, out_weight)
    far = {level: send(kv, xor(level)) for level in (5, 3, 4)}
    wl = unit
    for bit in (2, 1, 0):
        got = send(wl, xor(bit))
        up = ((y >> bit) & 1) == 1
        wl = jnp.concatenate([jnp.where(up, got, wl), jnp.where(up, wl, got)], axis=0)
    wl = after(wl, far, (3, 5))
    kv_y, wl = lax.optimization_barrier((kv, wl))
    far.update({level: send(kv_y, xor(level)) for level in (2, 1, 0)})
    marks = wl.reshape(NY, UNIT, 512)[:, WROWS:].reshape(NY * LROWS, 512)
    wl = jnp.concatenate([wl, send(marks, xor(3))], axis=0)
    wl = after(wl, far, (4,))
    wl1, wl3 = send(wl, along_x(1)), send(wl, along_x(-1))
    wl1 = after(wl1, far, (2,))
    wl2a, wl2b = send(wl1[:400], along_x(1)), send(wl3[400:], along_x(-1))
    pieces = (wl, wl1, wl3, wl2a, wl2b)

    early, late = (5, 3, 4, 2), (1, 0)
    state = first(early, place, pattern, queries, kv, [far[l] for l in early])
    mine = last(late, place, pattern, queries, state, pieces, [far[l] for l in late])
    other = send(mine, xor(3))
    keep, give = project(place, mine, other, pieces)
    got = send(give, lambda x, zl, y, zh, c: (x, zl, y, zh, 1 - c))
    part = (keep + got.astype(F32)).astype(BF16)
    total = 0.0
    for d in range(4):
        total += send(
            part[d], lambda x, zl, y, zh, c: (x, c, y, (zh + d) % NZH, zl)
        ).astype(F32)
    return total.astype(BF16)


def solution(mesh):
    in_specs = (
        P("ctx", "head"),
        P("ctx", "head"),
        P("ctx", "head"),
        P("ctx", None),
        P("head", "ctx"),
        P(),
    )
    return jax.shard_map(
        on_device, mesh=mesh, in_specs=in_specs, out_specs=P("ctx", "head"), check_vma=False
    )
```

```python
import functools

import jax
import jax.numpy as jnp
from jax import lax
from jax.experimental import pallas as pl
from jax.experimental.pallas import tpu as pltpu
from jax.sharding import PartitionSpec as P

HD = 128
BLK = 128
NX, NZL, NY, NZH, NC = 4, 2, 8, 4, 2
WROWS = 64
LROWS = 16
UNIT = WROWS + LROWS
HALF = 400
COST = 64
AXES = ("ctx", "head")
SCALE = HD**-0.5
F32 = jnp.float32
BF16 = jnp.bfloat16
VLIM = 16 << 20
HBM = pl.BlockSpec(memory_space=pltpu.HBM)
ANY = pl.BlockSpec(memory_space=pl.ANY)
SMEM = pl.BlockSpec(memory_space=pltpu.SMEM)
VMEM = pl.BlockSpec(memory_space=pltpu.VMEM)


def coords(i):
    ctx, head = divmod(i, NZH * NC)
    x, r = divmod(ctx, NZL * NY)
    zl, y = divmod(r, NY)
    zh, c = divmod(head, NC)
    return x, zl, y, zh, c


def flat(x, zl, y, zh, c):
    return ((x * NZL + zl) * NY + y) * (NZH * NC) + zh * NC + c


def send(a, to):
    pairs = [(i, flat(*to(*coords(i)))) for i in range(NX * NZL * NY * NZH * NC)]
    return lax.ppermute(a, AXES, pairs)


def xor(level):
    def to(x, zl, y, zh, c):
        ctx = ((x * NZL + zl) * NY + y) ^ (1 << level)
        x, r = divmod(ctx, NZL * NY)
        zl, y = divmod(r, NY)
        return x, zl, y, zh, c

    return to


def after(a, far, levels):
    if levels:
        a, done = lax.optimization_barrier((a, [far[l] for l in levels]))
        far.update(zip(levels, done, strict=True))
    return a


def in_hbm(a):
    return pltpu.with_memory_space_constraint(a, pltpu.HBM)


def params():
    return pltpu.CompilerParams(vmem_limit_bytes=VLIM)


def dot_nt(a, b):
    return lax.dot_general(a, b, (((1,), (1,)), ((), ())), preferred_element_type=F32)


def prepare_kernel(pool, keys, values, weight, kv, unit, pool_v, sem):
    copies = [
        pltpu.make_async_copy(weight, unit.at[pl.ds(0, WROWS)], sem.at[0]),
        pltpu.make_async_copy(pool, pool_v, sem.at[1]),
        pltpu.make_async_copy(keys, kv.at[pl.ds(0, 256)], sem.at[2]),
        pltpu.make_async_copy(values, kv.at[pl.ds(256, 256)], sem.at[3]),
    ]
    for copy in copies:
        copy.start()
    for copy in copies:
        copy.wait()
    pooled = [
        jnp.dot(pool_v[...], kv[r : r + 256, :], preferred_element_type=F32) for r in (0, 256)
    ]
    unit[WROWS:UNIT, :] = jnp.concatenate(pooled, axis=0).astype(BF16)


def prepare(pool, keys, values, weight):
    return pl.pallas_call(
        prepare_kernel,
        out_shape=(
            jax.ShapeDtypeStruct((512, 512), BF16),
            jax.ShapeDtypeStruct((UNIT, 512), BF16),
        ),
        in_specs=[HBM] * 4,
        out_specs=(VMEM,) * 2,
        scratch_shapes=[
            pltpu.VMEM((8, 256), BF16),
            pltpu.SemaphoreType.DMA((4,)),
        ],
        compiler_params=params(),
        name="prepare",
    )(*[in_hbm(a) for a in (pool, keys, values, weight)])


def softmax_step(state, q, ks, vs):
    scores = [dot_nt(q, k) * SCALE for k in ks]
    top = functools.reduce(jnp.maximum, [jnp.max(s, axis=1, keepdims=True) for s in scores])
    if state is not None:
        old_top, old_sum, old_acc = state
        top = jnp.maximum(top, old_top)
    weights = [jnp.exp(s - top) for s in scores]
    total = sum(jnp.sum(w, axis=1, keepdims=True) for w in weights)
    acc = sum(
        jnp.dot(w.astype(BF16), v, preferred_element_type=F32)
        for w, v in zip(weights, vs, strict=True)
    )
    if state is not None:
        fade = jnp.exp(old_top - top)
        total = total + old_sum * fade
        acc = acc + old_acc * fade
    return top, total, acc


def mark_rows(refs):
    rows = [b * UNIT + WROWS for b in range(NY)] + [NY * UNIT + b * LROWS for b in range(NY)]
    found = [(r, at) for r in refs[:3] for at in rows]
    found += [(refs[3], at) for at in rows if at < HALF]
    return found + [(refs[4], at - HALF) for at in rows if at >= HALF]


def landmarks(marks, cols):
    rows = marks[:, cols].astype(F32)
    groups = [rows[g * 8 : g * 8 + 8] for g in range(2 * NX * 16)]
    ks = jnp.concatenate(groups[0::2], axis=0)
    vs = jnp.concatenate(groups[1::2], axis=0)
    return ks.astype(BF16), vs.astype(BF16)


def attend_kernel(levels, own, carry, mark, final, place, pattern, q, *refs):
    refs = list(refs)
    own_ref = refs.pop(0) if own else None
    state_refs = [refs.pop(0) for _ in range(3)] if carry else None
    mark_refs = [refs.pop(0) for _ in range(5)] if mark else []
    far = [refs.pop(0) for _ in levels]
    outs = [refs.pop(0) for _ in range(1 if final else 3)]
    far_v = refs.pop(0) if levels else None
    mark_v = refs.pop(0) if mark else None
    sem = refs.pop(0)
    mark_sem = refs.pop(0) if mark else None
    copies = [pltpu.make_async_copy(r, far_v.at[i], sem.at[i]) for i, r in enumerate(far)]
    if mark:
        for i, (r, at) in enumerate(mark_rows(mark_refs)):
            dst = mark_v.at[pl.ds(i * LROWS, LROWS), :]
            copies.append(pltpu.make_async_copy(r.at[pl.ds(at, LROWS), :], dst, mark_sem.at[i]))
    for copy in copies:
        copy.start()
    for copy in copies:
        copy.wait()
    for h in range(4):
        cols = slice(h * HD, (h + 1) * HD)
        marks = landmarks(mark_v, cols) if mark else None
        for j in range(2):
            rows = slice(j * BLK, (j + 1) * BLK)
            ks, vs = [], []
            if own:
                ks.append(own_ref[0:256, cols])
                vs.append(own_ref[256:512, cols])
            if mark:
                ks.append(marks[0])
                vs.append(marks[1])
            for i, level in enumerate(levels):
                at = pl.multiple_of((pattern[1 + level, place[3] + j] & 1) * BLK, BLK)
                ks.append(far_v[i, pl.ds(at, BLK), cols])
                vs.append(far_v[i, pl.ds(256 + at, BLK), cols])
            state = None
            if carry:
                top, total, acc = state_refs
                first = slice(h * HD, h * HD + 1)
                state = (top[rows, first], total[rows, first], acc[rows, cols])
            m, s, a = softmax_step(state, q[rows, cols], ks, vs)
            if final:
                outs[0][rows, cols] = (a / s).astype(BF16)
            else:
                outs[0][rows, cols] = jnp.broadcast_to(m, (BLK, HD))
                outs[1][rows, cols] = jnp.broadcast_to(s, (BLK, HD))
                outs[2][rows, cols] = a


def attend(place, pattern, q, levels, far, own=None, state=None, mark=None, final=False, cost=1):
    args, specs = [place, pattern, q], [SMEM, SMEM, VMEM]
    if own is not None:
        args, specs = [*args, own], [*specs, VMEM]
    if state is not None:
        args, specs = [*args, *state], specs + [VMEM] * 3
    if mark is not None:
        args, specs = [*args, *mark], specs + [ANY] * 5
    args += [in_hbm(far[l]) for l in levels]
    specs += [HBM] * len(levels)
    scratch = [pltpu.VMEM((len(levels), 512, 512), BF16)] if levels else []
    if mark is not None:
        scratch.append(pltpu.VMEM((NX * 16 * LROWS, 512), BF16))
    scratch.append(pltpu.SemaphoreType.DMA((len(levels) + 1,)))
    if mark is not None:
        scratch.append(pltpu.SemaphoreType.DMA((NX * 16,)))
    count = 128 * len(levels) + 256 * (own is not None) + 512 * (mark is not None)
    return pl.pallas_call(
        functools.partial(
            attend_kernel, levels, own is not None, state is not None, mark is not None, final
        ),
        out_shape=jax.ShapeDtypeStruct((256, 512), BF16)
        if final
        else (jax.ShapeDtypeStruct((256, 512), F32),) * 3,
        in_specs=specs,
        out_specs=VMEM if final else (VMEM,) * 3,
        scratch_shapes=scratch,
        compiler_params=params(),
        name="attend",
        cost_estimate=pl.CostEstimate(
            flops=cost * 4 * 256 * 512 * count,
            bytes_accessed=4 << 20,
            transcendentals=1024 * count,
        ),
    )(*args)


def project_kernel(place, mine, other, w0, w1, w3, w2a, w2b, keep, give, w_v, sem):
    x, zh, same, y = place[0], place[1], place[2], place[4]
    chunks = ((0, ((w0, 0, 768),)), (1, ((w1, 0, 768),)), (3, ((w3, 0, 768),)))
    chunks += ((2, ((w2a, 0, HALF), (w2b, HALF, 768))),)
    copies = []
    for i, (_, pieces) in enumerate(chunks):
        for p in range(NY):
            at = y ^ (4 * (p & 1) + (p & 2) + (p >> 2))
            dst = w_v.at[i, pl.ds(pl.multiple_of(at * WROWS, WROWS), WROWS), :]
            [src] = [
                r.at[pl.ds(p * UNIT - lo, WROWS), :] for r, lo, hi in pieces if lo <= p * UNIT < hi
            ]
            copies.append(pltpu.make_async_copy(src, dst, sem.at[i * NY + p]))
    for copy in copies:
        copy.start()
    swap = same == 0
    a, b = mine[...], other[...]
    kept = jnp.where(swap, b, a)
    given = jnp.where(swap, a, b)
    for i, (shift, _) in enumerate(chunks):
        for copy in copies[i * NY : (i + 1) * NY]:
            copy.wait()
        d = (x + 2 * NX - shift - zh) & 3
        give[d] = dot_nt(given, w_v[i]).astype(BF16)
        keep[d] = dot_nt(kept, w_v[i])


def project(place, mine, other, wl):
    return pl.pallas_call(
        project_kernel,
        out_shape=(
            jax.ShapeDtypeStruct((4, 256, 512), F32),
            jax.ShapeDtypeStruct((4, 256, 512), BF16),
        ),
        in_specs=[SMEM] + [VMEM] * 2 + [ANY] * 5,
        out_specs=(VMEM,) * 2,
        scratch_shapes=[
            pltpu.VMEM((NX, NY * WROWS, 512), BF16),
            pltpu.SemaphoreType.DMA((NX * NY,)),
        ],
        compiler_params=params(),
        name="project",
        cost_estimate=pl.CostEstimate(
            flops=2 * 512 * 512 * 2048, bytes_accessed=6 << 20, transcendentals=0
        ),
    )(place, mine, other, *wl)


def join_kernel(a, b, out):
    n = a.shape[0]
    out[0:n, :] = a[...]
    out[n:, :] = b[...]


def join(a, b):
    return pl.pallas_call(
        join_kernel,
        out_shape=jax.ShapeDtypeStruct((a.shape[0] + b.shape[0], 512), BF16),
        in_specs=[VMEM] * 2,
        out_specs=VMEM,
        compiler_params=params(),
        name="join",
    )(a, b)


def pick_kernel(a, out):
    for p in range(NY):
        out[p * LROWS : (p + 1) * LROWS, :] = a[p * UNIT + WROWS : (p + 1) * UNIT, :]


def pick(a):
    return pl.pallas_call(
        pick_kernel,
        out_shape=jax.ShapeDtypeStruct((NY * LROWS, 512), BF16),
        in_specs=[VMEM],
        out_specs=VMEM,
        compiler_params=params(),
        name="pick",
    )(a)


def combine_kernel(keep, got, *outs):
    for d in range(4):
        outs[d][...] = (keep[d] + got[d].astype(F32)).astype(BF16)


def combine(keep, got):
    return pl.pallas_call(
        combine_kernel,
        out_shape=(jax.ShapeDtypeStruct((256, 512), BF16),) * 4,
        in_specs=[VMEM] * 2,
        out_specs=(VMEM,) * 4,
        compiler_params=params(),
        name="combine",
    )(keep, got)


def along_x(k):
    return lambda x, zl, y, zh, c: ((x + k) % NX, zl, y, zh, c)


def on_device(queries, keys, values, pool_weight, out_weight, pattern):
    ctx, head = lax.axis_index("ctx"), lax.axis_index("head")
    zl, c = (ctx >> 3) & 1, head & 1
    place = jnp.stack([ctx >> 4, head >> 1, (zl == c).astype(jnp.int32), ctx * 2, ctx & 7])

    kv, wl = prepare(pool_weight, keys, values, out_weight.T)
    step = functools.partial(attend, place, pattern.T, queries)
    far = {level: send(kv, xor(level)) for level in (5, 3)}
    wl = join(wl, send(wl, xor(2)))
    kv, wl = lax.optimization_barrier((kv, wl))
    far.update({level: send(kv, xor(level)) for level in (4, 0)})
    wl = join(wl, send(wl, xor(1)))
    wl = after(wl, far, (5, 3))
    kv, wl = lax.optimization_barrier((kv, wl))
    far.update({level: send(kv, xor(level)) for level in (2, 1)})
    wl = join(wl, send(wl, xor(0)))
    marks = after(pick(wl), far, (4, 0))
    state = step((5, 3, 4, 0), far, own=kv)
    wl = join(wl, send(marks, xor(3)))
    wl1, wl3 = send(wl, along_x(1)), send(wl, along_x(-1))
    state = step((2,), far, state=state, cost=COST)
    wl1, wl3, state = lax.optimization_barrier((wl1, wl3, state))
    wl2a, wl2b = send(wl1[:HALF], along_x(1)), send(wl3[HALF:], along_x(-1))
    pieces = (wl, wl1, wl3, wl2a, wl2b)
    state = step((1,), far, state=state, cost=COST)
    mine = step((), far, state=state, mark=pieces, final=True)
    other = send(mine, xor(3))
    keep, give = project(place, mine, other, pieces)
    got = send(give, lambda x, zl, y, zh, c: (x, zl, y, zh, 1 - c))
    part = combine(keep, got)
    total = 0.0
    for d in range(4):
        total += send(
            part[d], lambda x, zl, y, zh, c: (x, c, y, (zh + d) % NZH, zl)
        ).astype(F32)
    return total.astype(BF16)


def solution(mesh):
    in_specs = (
        P("ctx", "head"),
        P("ctx", "head"),
        P("ctx", "head"),
        P("ctx", None),
        P("head", "ctx"),
        P(),
    )
    return jax.shard_map(
        on_device, mesh=mesh, in_specs=in_specs, out_specs=P("ctx", "head"), check_vma=False
    )
```

```python
import functools

import jax
import jax.numpy as jnp
from jax import lax
from jax.experimental import pallas as pl
from jax.experimental.pallas import tpu as pltpu
from jax.sharding import PartitionSpec as P

HD = 128
BLK = 128
NX, NZL, NY, NZH, NC = 4, 2, 8, 4, 2
WROWS = 64
LROWS = 16
UNIT = WROWS + LROWS
HALF = 400
COST = 64
COST0 = 64
COST1 = 0
AXES = ("ctx", "head")
SCALE = HD**-0.5
F32 = jnp.float32
BF16 = jnp.bfloat16
VLIM = 16 << 20
HBM = pl.BlockSpec(memory_space=pltpu.HBM)
ANY = pl.BlockSpec(memory_space=pl.ANY)
SMEM = pl.BlockSpec(memory_space=pltpu.SMEM)
VMEM = pl.BlockSpec(memory_space=pltpu.VMEM)


def coords(i):
    ctx, head = divmod(i, NZH * NC)
    x, r = divmod(ctx, NZL * NY)
    zl, y = divmod(r, NY)
    zh, c = divmod(head, NC)
    return x, zl, y, zh, c


def flat(x, zl, y, zh, c):
    return ((x * NZL + zl) * NY + y) * (NZH * NC) + zh * NC + c


def send(a, to):
    pairs = [(i, flat(*to(*coords(i)))) for i in range(NX * NZL * NY * NZH * NC)]
    return lax.ppermute(a, AXES, pairs)


def xor(level):
    def to(x, zl, y, zh, c):
        ctx = ((x * NZL + zl) * NY + y) ^ (1 << level)
        x, r = divmod(ctx, NZL * NY)
        zl, y = divmod(r, NY)
        return x, zl, y, zh, c

    return to


def after(a, far, levels):
    if levels:
        a, done = lax.optimization_barrier((a, [far[l] for l in levels]))
        far.update(zip(levels, done, strict=True))
    return a


def in_hbm(a):
    return pltpu.with_memory_space_constraint(a, pltpu.HBM)


def params():
    return pltpu.CompilerParams(vmem_limit_bytes=VLIM)


def dot_nt(a, b):
    return lax.dot_general(a, b, (((1,), (1,)), ((), ())), preferred_element_type=F32)


def prepare_kernel(pool, keys, values, weight, unit, pool_v, kv_v, sem):
    copies = [
        pltpu.make_async_copy(weight, unit.at[pl.ds(0, WROWS)], sem.at[0]),
        pltpu.make_async_copy(pool, pool_v, sem.at[1]),
        pltpu.make_async_copy(keys, kv_v.at[pl.ds(0, 256)], sem.at[2]),
        pltpu.make_async_copy(values, kv_v.at[pl.ds(256, 256)], sem.at[3]),
    ]
    for copy in copies:
        copy.start()
    for copy in copies:
        copy.wait()
    pooled = [
        jnp.dot(pool_v[...], kv_v[r : r + 256, :], preferred_element_type=F32) for r in (0, 256)
    ]
    unit[WROWS:UNIT, :] = jnp.concatenate(pooled, axis=0).astype(BF16)


def prepare(pool, keys, values, weight):
    return pl.pallas_call(
        prepare_kernel,
        out_shape=jax.ShapeDtypeStruct((UNIT, 512), BF16),
        in_specs=[HBM] * 4,
        out_specs=VMEM,
        scratch_shapes=[
            pltpu.VMEM((8, 256), BF16),
            pltpu.VMEM((512, 512), BF16),
            pltpu.SemaphoreType.DMA((4,)),
        ],
        compiler_params=params(),
        name="prepare",
    )(*[in_hbm(a) for a in (pool, keys, values, weight)])


def stack_kernel(keys, values, kv, sem):
    copies = [
        pltpu.make_async_copy(keys, kv.at[pl.ds(0, 256)], sem.at[0]),
        pltpu.make_async_copy(values, kv.at[pl.ds(256, 256)], sem.at[1]),
    ]
    for copy in copies:
        copy.start()
    for copy in copies:
        copy.wait()


def stack(keys, values):
    return pl.pallas_call(
        stack_kernel,
        out_shape=jax.ShapeDtypeStruct((512, 512), BF16),
        in_specs=[HBM] * 2,
        out_specs=VMEM,
        scratch_shapes=[pltpu.SemaphoreType.DMA((2,))],
        compiler_params=params(),
        name="stack",
    )(in_hbm(keys), in_hbm(values))


def softmax_step(state, q, ks, vs):
    scores = [dot_nt(q, k) * SCALE for k in ks]
    top = functools.reduce(jnp.maximum, [jnp.max(s, axis=1, keepdims=True) for s in scores])
    if state is not None:
        old_top, old_sum, old_acc = state
        top = jnp.maximum(top, old_top)
    weights = [jnp.exp(s - top) for s in scores]
    total = sum(jnp.sum(w, axis=1, keepdims=True) for w in weights)
    acc = sum(
        jnp.dot(w.astype(BF16), v, preferred_element_type=F32)
        for w, v in zip(weights, vs, strict=True)
    )
    if state is not None:
        fade = jnp.exp(old_top - top)
        total = total + old_sum * fade
        acc = acc + old_acc * fade
    return top, total, acc


def mark_starts(lo, hi):
    rows = [b * UNIT + WROWS for b in range(NY)] + [NY * UNIT + b * LROWS for b in range(NY)]
    return tuple(r - lo for r in rows if lo <= r < hi)


def landmarks(marks, cols):
    rows = marks[:, cols].astype(F32)
    groups = [rows[g : g + 8] for g in range(0, rows.shape[0], 8)]
    ks = jnp.concatenate(groups[0::2], axis=0)
    vs = jnp.concatenate(groups[1::2], axis=0)
    return ks.astype(BF16), vs.astype(BF16)


def attend_kernel(levels, own, carry, mark, final, token, place, pattern, q, *refs):
    refs = list(refs)
    own_ref = refs.pop(0) if own else None
    state_refs = [refs.pop(0) for _ in range(3)] if carry else None
    mark_refs = [refs.pop(0) for _ in mark]
    far = [refs.pop(0) for _ in levels]
    if token:
        refs.pop(0)
    outs = [refs.pop(0) for _ in range(1 if final else 3)]
    far_v = refs.pop(0) if levels else None
    mark_v = refs.pop(0) if mark else None
    sem = refs.pop(0)
    mark_sem = refs.pop(0) if mark else None
    copies = [pltpu.make_async_copy(r, far_v.at[i], sem.at[i]) for i, r in enumerate(far)]
    if mark:
        rows = [(r, at) for r, starts in zip(mark_refs, mark, strict=True) for at in starts]
        for i, (r, at) in enumerate(rows):
            dst = mark_v.at[pl.ds(i * LROWS, LROWS), :]
            copies.append(pltpu.make_async_copy(r.at[pl.ds(at, LROWS), :], dst, mark_sem.at[i]))
    for copy in copies:
        copy.start()
    for copy in copies:
        copy.wait()
    for h in range(4):
        cols = slice(h * HD, (h + 1) * HD)
        marks = landmarks(mark_v, cols) if mark else None
        for j in range(2):
            rows = slice(j * BLK, (j + 1) * BLK)
            ks, vs = [], []
            if own:
                ks.append(own_ref[0:256, cols])
                vs.append(own_ref[256:512, cols])
            if mark:
                ks.append(marks[0])
                vs.append(marks[1])
            for i, level in enumerate(levels):
                at = pl.multiple_of((pattern[1 + level, place[2] + j] & 1) * BLK, BLK)
                ks.append(far_v[i, pl.ds(at, BLK), cols])
                vs.append(far_v[i, pl.ds(256 + at, BLK), cols])
            state = None
            if carry:
                top, total, acc = state_refs
                first = slice(h * HD, h * HD + 1)
                state = (top[rows, first], total[rows, first], acc[rows, cols])
            m, s, a = softmax_step(state, q[rows, cols], ks, vs)
            if final:
                outs[0][rows, cols] = (a / s).astype(BF16)
            else:
                outs[0][rows, cols] = jnp.broadcast_to(m, (BLK, HD))
                outs[1][rows, cols] = jnp.broadcast_to(s, (BLK, HD))
                outs[2][rows, cols] = a


def attend(place, pattern, q, levels, far, own=None, state=None, mark=(), final=False, cost=1, token=None):
    args, specs = [place, pattern, q], [SMEM, SMEM, VMEM]
    if own is not None:
        args, specs = [*args, own], [*specs, VMEM]
    if state is not None:
        args, specs = [*args, *state], specs + [VMEM] * 3
    args += [a for a, _ in mark]
    specs += [ANY] * len(mark)
    args += [in_hbm(far[l]) for l in levels]
    specs += [HBM] * len(levels)
    if token is not None:
        args, specs = [*args, token], [*specs, ANY]
    scratch = [pltpu.VMEM((len(levels), 512, 512), BF16)] if levels else []
    groups = sum(len(starts) for _, starts in mark)
    if mark:
        scratch.append(pltpu.VMEM((groups * LROWS, 512), BF16))
    scratch.append(pltpu.SemaphoreType.DMA((len(levels) + 1,)))
    if mark:
        scratch.append(pltpu.SemaphoreType.DMA((groups,)))
    count = 128 * len(levels) + 256 * (own is not None) + 8 * groups
    return pl.pallas_call(
        functools.partial(
            attend_kernel,
            levels,
            own is not None,
            state is not None,
            tuple(starts for _, starts in mark),
            final,
            token is not None,
        ),
        out_shape=jax.ShapeDtypeStruct((256, 512), BF16)
        if final
        else (jax.ShapeDtypeStruct((256, 512), F32),) * 3,
        in_specs=specs,
        out_specs=VMEM if final else (VMEM,) * 3,
        scratch_shapes=scratch,
        compiler_params=params(),
        name="attend",
        cost_estimate=pl.CostEstimate(
            flops=cost * 4 * 256 * 512 * count,
            bytes_accessed=4 << 20,
            transcendentals=1024 * count,
        ),
    )(*args)


def pack_kernel(place, w0, w1, w2a, w2b, w3, out):
    y = place[3]
    chunks = (((w0, 0, 768),), ((w1, 0, 768),), ((w2a, 0, HALF), (w2b, HALF, 768)))
    chunks += (((w3, 0, 768),),)
    for i, pieces in enumerate(chunks):
        for p in range(NY):
            at = pl.multiple_of((y ^ (4 * (p & 1) + (p & 2) + (p >> 2))) * WROWS, WROWS)
            [(ref, lo)] = [(r, lo) for r, lo, hi in pieces if lo <= p * UNIT < hi]
            out[i, pl.ds(at, WROWS), :] = ref[p * UNIT - lo : p * UNIT - lo + WROWS, :]


def pack(place, wl):
    return pl.pallas_call(
        pack_kernel,
        out_shape=jax.ShapeDtypeStruct((NX, NY * WROWS, 512), BF16),
        in_specs=[SMEM] + [VMEM] * 5,
        out_specs=VMEM,
        compiler_params=params(),
        name="pack",
    )(place, *wl)


def project_kernel(place, mine, got1, got2, w_mine, w_other, *outs):
    step, same = place[0], place[1] == 1
    a, b = mine[...], got1[...]
    first = jnp.where(same, a, b)
    second = jnp.where(same, b, got2[...])
    for d in range(4):
        shift = (step - d) & 3
        outs[d][...] = (dot_nt(first, w_mine[shift]) + dot_nt(second, w_other[shift])).astype(BF16)


def project(place, mine, got1, got2, w_mine, w_other):
    return pl.pallas_call(
        project_kernel,
        out_shape=(jax.ShapeDtypeStruct((256, 512), BF16),) * 4,
        in_specs=[SMEM] + [VMEM] * 5,
        out_specs=(VMEM,) * 4,
        compiler_params=params(),
        name="project",
        cost_estimate=pl.CostEstimate(
            flops=2 * 512 * 512 * 2048, bytes_accessed=6 << 20, transcendentals=0
        ),
    )(place, mine, got1, got2, w_mine, w_other)


def join_kernel(a, b, out):
    n = a.shape[0]
    out[0:n, :] = a[...]
    out[n:, :] = b[...]


def join(a, b):
    return pl.pallas_call(
        join_kernel,
        out_shape=jax.ShapeDtypeStruct((a.shape[0] + b.shape[0], 512), BF16),
        in_specs=[VMEM] * 2,
        out_specs=VMEM,
        compiler_params=params(),
        name="join",
    )(a, b)


def arrived_kernel(*refs):
    refs[-1][...] = jnp.zeros_like(refs[-1])


def arrived(cost, *arrays):
    return pl.pallas_call(
        arrived_kernel,
        out_shape=jax.ShapeDtypeStruct((8, 128), F32),
        in_specs=[HBM] * len(arrays),
        out_specs=VMEM,
        compiler_params=params(),
        name="arrived",
        cost_estimate=pl.CostEstimate(flops=cost << 27, bytes_accessed=4 << 20, transcendentals=0),
    )(*[in_hbm(a) for a in arrays])


def pick_kernel(a, out):
    for p in range(NY):
        out[p * LROWS : (p + 1) * LROWS, :] = a[p * UNIT + WROWS : (p + 1) * UNIT, :]


def pick(a):
    return pl.pallas_call(
        pick_kernel,
        out_shape=jax.ShapeDtypeStruct((NY * LROWS, 512), BF16),
        in_specs=[VMEM],
        out_specs=VMEM,
        compiler_params=params(),
        name="pick",
    )(a)


def along_x(k):
    return lambda x, zl, y, zh, c: ((x + k) % NX, zl, y, zh, c)


def to_first(x, zl, y, zh, c):
    return (x, zl, y, zh, 1 - c) if zl != c else (x, 1 - zl, y, zh, c)


def to_second(x, zl, y, zh, c):
    return (x, 1 - zl, y, zh, 1 - c) if zl != c else (x, zl, y, zh, c)


def on_device(queries, keys, values, pool_weight, out_weight, pattern):
    ctx, head = lax.axis_index("ctx"), lax.axis_index("head")
    same = (((ctx >> 3) ^ head) & 1) ^ 1
    place = jnp.stack([(ctx >> 4) + NX - (head >> 1), same, ctx * 2, ctx & 7])

    wl = prepare(pool_weight, keys, values, out_weight.T)
    step = functools.partial(attend, place, pattern.T, queries)
    keys, values, wl = lax.optimization_barrier((keys, values, wl))
    kv = stack(keys, values)
    wl = join(wl, send(wl, xor(2)))
    kv, wl = lax.optimization_barrier((kv, wl))
    far = {level: send(kv, xor(level)) for level in (3, 5)}
    wl = join(wl, send(wl, xor(1)))
    kv, wl = lax.optimization_barrier((kv, wl))
    far[4] = send(kv, xor(4))
    wl = join(wl, send(wl, xor(0)))
    marks = pick(wl)
    kv, marks = lax.optimization_barrier((kv, marks))
    far[2] = send(kv, xor(2))
    wl = join(wl, send(marks, xor(3)))
    wl1, wl3 = send(wl, along_x(1)), send(wl, along_x(-1))
    every = mark_starts(0, 768)
    token = arrived(COST0, far[3], far[5], far[4])
    kv, token, wl = lax.optimization_barrier((kv, token, wl))
    far.update({level: send(kv, xor(level)) for level in (1, 0)})
    state = step((3, 5, 4, 2), far, own=kv, mark=[(wl, every)], token=token, cost=COST)
    wl1, wl3, state = lax.optimization_barrier((wl1, wl3, state))
    wl2a, wl2b = send(wl1[:HALF], along_x(1)), send(wl3[HALF:], along_x(-1))
    state = step((), far, state=state, mark=[(wl1, every), (wl3, every)])
    rest = [(wl2a, mark_starts(0, HALF)), (wl2b, mark_starts(HALF, 768))]
    late, state = lax.optimization_barrier(((far[1], far[0]), state))
    far[1], far[0] = late
    token = arrived(COST1, *late)
    pieces = (wl, wl1, wl2a, wl2b, wl3)
    pieces, token, state = lax.optimization_barrier((pieces, token, state))
    mine = step((1, 0), far, state=state, mark=rest, final=True, token=token)
    w_mine = pack(place, pieces)
    w_other = send(w_mine, lambda x, zl, y, zh, c: (x, zl, y, zh, 1 - c))
    part = project(place, mine, send(mine, to_first), send(mine, to_second), w_mine, w_other)
    total = 0.0
    for d in range(4):
        total += send(
            part[d], lambda x, zl, y, zh, c: (x, c, y, (zh + d) % NZH, zl)
        ).astype(F32)
    return total.astype(BF16)


def solution(mesh):
    in_specs = (
        P("ctx", "head"),
        P("ctx", "head"),
        P("ctx", "head"),
        P("ctx", None),
        P("head", "ctx"),
        P(),
    )
    return jax.shard_map(
        on_device, mesh=mesh, in_specs=in_specs, out_specs=P("ctx", "head"), check_vma=False
    )
```

```python
import functools

import jax
import jax.numpy as jnp
from jax import lax
from jax.experimental import pallas as pl
from jax.experimental.pallas import tpu as pltpu
from jax.sharding import PartitionSpec as P

HD = 128
BLK = 128
NX, NZL, NY, NZH, NC = 4, 2, 8, 4, 2
WROWS = 64
LROWS = 16
UNIT = WROWS + LROWS
HALF = 400
COST = 1
COST0 = 64
COST2 = 1
COST3 = 0
COST1 = 0
AXES = ("ctx", "head")
SCALE = HD**-0.5
F32 = jnp.float32
BF16 = jnp.bfloat16
VLIM = 16 << 20
HBM = pl.BlockSpec(memory_space=pltpu.HBM)
ANY = pl.BlockSpec(memory_space=pl.ANY)
SMEM = pl.BlockSpec(memory_space=pltpu.SMEM)
VMEM = pl.BlockSpec(memory_space=pltpu.VMEM)


def coords(i):
    ctx, head = divmod(i, NZH * NC)
    x, r = divmod(ctx, NZL * NY)
    zl, y = divmod(r, NY)
    zh, c = divmod(head, NC)
    return x, zl, y, zh, c


def flat(x, zl, y, zh, c):
    return ((x * NZL + zl) * NY + y) * (NZH * NC) + zh * NC + c


def send(a, to):
    pairs = [(i, flat(*to(*coords(i)))) for i in range(NX * NZL * NY * NZH * NC)]
    return lax.ppermute(a, AXES, pairs)


def xor(level):
    def to(x, zl, y, zh, c):
        ctx = ((x * NZL + zl) * NY + y) ^ (1 << level)
        x, r = divmod(ctx, NZL * NY)
        zl, y = divmod(r, NY)
        return x, zl, y, zh, c

    return to


def after(a, far, levels):
    if levels:
        a, done = lax.optimization_barrier((a, [far[l] for l in levels]))
        far.update(zip(levels, done, strict=True))
    return a


def in_hbm(a):
    return pltpu.with_memory_space_constraint(a, pltpu.HBM)


def params():
    return pltpu.CompilerParams(vmem_limit_bytes=VLIM)


def dot_nt(a, b):
    return lax.dot_general(a, b, (((1,), (1,)), ((), ())), preferred_element_type=F32)


def prepare_kernel(pool, keys, values, weight, unit, pool_v, kv_v, sem):
    copies = [
        pltpu.make_async_copy(weight, unit.at[pl.ds(0, WROWS)], sem.at[0]),
        pltpu.make_async_copy(pool, pool_v, sem.at[1]),
        pltpu.make_async_copy(keys, kv_v.at[pl.ds(0, 256)], sem.at[2]),
        pltpu.make_async_copy(values, kv_v.at[pl.ds(256, 256)], sem.at[3]),
    ]
    for copy in copies:
        copy.start()
    for copy in copies:
        copy.wait()
    pooled = [
        jnp.dot(pool_v[...], kv_v[r : r + 256, :], preferred_element_type=F32) for r in (0, 256)
    ]
    unit[WROWS:UNIT, :] = jnp.concatenate(pooled, axis=0).astype(BF16)


def prepare(pool, keys, values, weight):
    return pl.pallas_call(
        prepare_kernel,
        out_shape=jax.ShapeDtypeStruct((UNIT, 512), BF16),
        in_specs=[HBM] * 4,
        out_specs=VMEM,
        scratch_shapes=[
            pltpu.VMEM((8, 256), BF16),
            pltpu.VMEM((512, 512), BF16),
            pltpu.SemaphoreType.DMA((4,)),
        ],
        compiler_params=params(),
        name="prepare",
    )(*[in_hbm(a) for a in (pool, keys, values, weight)])


def stack_kernel(keys, values, kv, sem):
    copies = [
        pltpu.make_async_copy(keys, kv.at[pl.ds(0, 256)], sem.at[0]),
        pltpu.make_async_copy(values, kv.at[pl.ds(256, 256)], sem.at[1]),
    ]
    for copy in copies:
        copy.start()
    for copy in copies:
        copy.wait()


def stack(keys, values):
    return pl.pallas_call(
        stack_kernel,
        out_shape=jax.ShapeDtypeStruct((512, 512), BF16),
        in_specs=[HBM] * 2,
        out_specs=VMEM,
        scratch_shapes=[pltpu.SemaphoreType.DMA((2,))],
        compiler_params=params(),
        name="stack",
    )(in_hbm(keys), in_hbm(values))


def softmax_step(state, q, ks, vs):
    scores = [dot_nt(q, k) * SCALE for k in ks]
    top = functools.reduce(jnp.maximum, [jnp.max(s, axis=1, keepdims=True) for s in scores])
    if state is not None:
        old_top, old_sum, old_acc = state
        top = jnp.maximum(top, old_top)
    weights = [jnp.exp(s - top) for s in scores]
    total = sum(jnp.sum(w, axis=1, keepdims=True) for w in weights)
    acc = sum(
        jnp.dot(w.astype(BF16), v, preferred_element_type=F32)
        for w, v in zip(weights, vs, strict=True)
    )
    if state is not None:
        fade = jnp.exp(old_top - top)
        total = total + old_sum * fade
        acc = acc + old_acc * fade
    return top, total, acc


def mark_starts(lo, hi):
    rows = [b * UNIT + WROWS for b in range(NY)] + [NY * UNIT + b * LROWS for b in range(NY)]
    return tuple(r - lo for r in rows if lo <= r < hi)


def landmarks(marks, cols):
    rows = marks[:, cols].astype(F32)
    groups = [rows[g : g + 8] for g in range(0, rows.shape[0], 8)]
    ks = jnp.concatenate(groups[0::2], axis=0)
    vs = jnp.concatenate(groups[1::2], axis=0)
    return ks.astype(BF16), vs.astype(BF16)


def attend_kernel(levels, own, carry, mark, final, token, place, pattern, q, *refs):
    refs = list(refs)
    own_ref = refs.pop(0) if own else None
    state_refs = [refs.pop(0) for _ in range(3)] if carry else None
    mark_refs = [refs.pop(0) for _ in mark]
    far = [refs.pop(0) for _ in levels]
    if token:
        refs.pop(0)
    outs = [refs.pop(0) for _ in range(1 if final else 3)]
    far_v = refs.pop(0) if levels else None
    mark_v = refs.pop(0) if mark else None
    sem = refs.pop(0)
    mark_sem = refs.pop(0) if mark else None
    copies = [pltpu.make_async_copy(r, far_v.at[i], sem.at[i]) for i, r in enumerate(far)]
    if mark:
        rows = [(r, at) for r, starts in zip(mark_refs, mark, strict=True) for at in starts]
        for i, (r, at) in enumerate(rows):
            dst = mark_v.at[pl.ds(i * LROWS, LROWS), :]
            copies.append(pltpu.make_async_copy(r.at[pl.ds(at, LROWS), :], dst, mark_sem.at[i]))
    for copy in copies:
        copy.start()
    for copy in copies:
        copy.wait()
    for h in range(4):
        cols = slice(h * HD, (h + 1) * HD)
        marks = landmarks(mark_v, cols) if mark else None
        for j in range(2):
            rows = slice(j * BLK, (j + 1) * BLK)
            ks, vs = [], []
            if own:
                ks.append(own_ref[0:256, cols])
                vs.append(own_ref[256:512, cols])
            if mark:
                ks.append(marks[0])
                vs.append(marks[1])
            for i, level in enumerate(levels):
                at = pl.multiple_of((pattern[1 + level, place[2] + j] & 1) * BLK, BLK)
                ks.append(far_v[i, pl.ds(at, BLK), cols])
                vs.append(far_v[i, pl.ds(256 + at, BLK), cols])
            state = None
            if carry:
                top, total, acc = state_refs
                first = slice(h * HD, h * HD + 1)
                state = (top[rows, first], total[rows, first], acc[rows, cols])
            m, s, a = softmax_step(state, q[rows, cols], ks, vs)
            if final:
                outs[0][rows, cols] = (a / s).astype(BF16)
            else:
                outs[0][rows, cols] = jnp.broadcast_to(m, (BLK, HD))
                outs[1][rows, cols] = jnp.broadcast_to(s, (BLK, HD))
                outs[2][rows, cols] = a


def attend(place, pattern, q, levels, far, own=None, state=None, mark=(), final=False, cost=1, token=None):
    args, specs = [place, pattern, q], [SMEM, SMEM, VMEM]
    if own is not None:
        args, specs = [*args, own], [*specs, VMEM]
    if state is not None:
        args, specs = [*args, *state], specs + [VMEM] * 3
    args += [a for a, _ in mark]
    specs += [ANY] * len(mark)
    args += [in_hbm(far[l]) for l in levels]
    specs += [HBM] * len(levels)
    if token is not None:
        args, specs = [*args, token], [*specs, ANY]
    scratch = [pltpu.VMEM((len(levels), 512, 512), BF16)] if levels else []
    groups = sum(len(starts) for _, starts in mark)
    if mark:
        scratch.append(pltpu.VMEM((groups * LROWS, 512), BF16))
    scratch.append(pltpu.SemaphoreType.DMA((len(levels) + 1,)))
    if mark:
        scratch.append(pltpu.SemaphoreType.DMA((groups,)))
    count = 128 * len(levels) + 256 * (own is not None) + 8 * groups
    return pl.pallas_call(
        functools.partial(
            attend_kernel,
            levels,
            own is not None,
            state is not None,
            tuple(starts for _, starts in mark),
            final,
            token is not None,
        ),
        out_shape=jax.ShapeDtypeStruct((256, 512), BF16)
        if final
        else (jax.ShapeDtypeStruct((256, 512), F32),) * 3,
        in_specs=specs,
        out_specs=VMEM if final else (VMEM,) * 3,
        scratch_shapes=scratch,
        compiler_params=params(),
        name="attend",
        cost_estimate=pl.CostEstimate(
            flops=cost * 4 * 256 * 512 * count,
            bytes_accessed=4 << 20,
            transcendentals=1024 * count,
        ),
    )(*args)


def pack_kernel(place, w0, w1, w2a, w2b, w3, out):
    y = place[3]
    chunks = (((w0, 0, 768),), ((w1, 0, 768),), ((w2a, 0, HALF), (w2b, HALF, 768)))
    chunks += (((w3, 0, 768),),)
    for i, pieces in enumerate(chunks):
        for p in range(NY):
            at = pl.multiple_of((y ^ (4 * (p & 1) + (p & 2) + (p >> 2))) * WROWS, WROWS)
            [(ref, lo)] = [(r, lo) for r, lo, hi in pieces if lo <= p * UNIT < hi]
            out[i, pl.ds(at, WROWS), :] = ref[p * UNIT - lo : p * UNIT - lo + WROWS, :]


def pack(place, wl):
    return pl.pallas_call(
        pack_kernel,
        out_shape=jax.ShapeDtypeStruct((NX, NY * WROWS, 512), BF16),
        in_specs=[SMEM] + [VMEM] * 5,
        out_specs=VMEM,
        compiler_params=params(),
        name="pack",
    )(place, *wl)


def project_kernel(place, mine, got1, got2, w_mine, w_other, *outs):
    step, same = place[0], place[1] == 1
    a, b = mine[...], got1[...]
    first = jnp.where(same, a, b)
    second = jnp.where(same, b, got2[...])
    for d in range(4):
        shift = (step - d) & 3
        outs[d][...] = (dot_nt(first, w_mine[shift]) + dot_nt(second, w_other[shift])).astype(BF16)


def project(place, mine, got1, got2, w_mine, w_other):
    return pl.pallas_call(
        project_kernel,
        out_shape=(jax.ShapeDtypeStruct((256, 512), BF16),) * 4,
        in_specs=[SMEM] + [VMEM] * 5,
        out_specs=(VMEM,) * 4,
        compiler_params=params(),
        name="project",
        cost_estimate=pl.CostEstimate(
            flops=2 * 512 * 512 * 2048, bytes_accessed=6 << 20, transcendentals=0
        ),
    )(place, mine, got1, got2, w_mine, w_other)


def join_kernel(a, b, out):
    n = a.shape[0]
    out[0:n, :] = a[...]
    out[n:, :] = b[...]


def join(a, b):
    return pl.pallas_call(
        join_kernel,
        out_shape=jax.ShapeDtypeStruct((a.shape[0] + b.shape[0], 512), BF16),
        in_specs=[VMEM] * 2,
        out_specs=VMEM,
        compiler_params=params(),
        name="join",
    )(a, b)


def arrived_kernel(*refs):
    refs[-1][...] = jnp.zeros_like(refs[-1])


def arrived(cost, *arrays):
    return pl.pallas_call(
        arrived_kernel,
        out_shape=jax.ShapeDtypeStruct((8, 128), F32),
        in_specs=[HBM] * len(arrays),
        out_specs=VMEM,
        compiler_params=params(),
        name="arrived",
        cost_estimate=pl.CostEstimate(flops=cost << 27, bytes_accessed=4 << 20, transcendentals=0),
    )(*[in_hbm(a) for a in arrays])


def pick_kernel(a, out):
    for p in range(NY):
        out[p * LROWS : (p + 1) * LROWS, :] = a[p * UNIT + WROWS : (p + 1) * UNIT, :]


def pick(a):
    return pl.pallas_call(
        pick_kernel,
        out_shape=jax.ShapeDtypeStruct((NY * LROWS, 512), BF16),
        in_specs=[VMEM],
        out_specs=VMEM,
        compiler_params=params(),
        name="pick",
    )(a)


def along_x(k):
    return lambda x, zl, y, zh, c: ((x + k) % NX, zl, y, zh, c)


def to_first(x, zl, y, zh, c):
    return (x, zl, y, zh, 1 - c) if zl != c else (x, 1 - zl, y, zh, c)


def to_second(x, zl, y, zh, c):
    return (x, 1 - zl, y, zh, 1 - c) if zl != c else (x, zl, y, zh, c)


def on_device(queries, keys, values, pool_weight, out_weight, pattern):
    ctx, head = lax.axis_index("ctx"), lax.axis_index("head")
    same = (((ctx >> 3) ^ head) & 1) ^ 1
    place = jnp.stack([(ctx >> 4) + NX - (head >> 1), same, ctx * 2, ctx & 7])

    wl = prepare(pool_weight, keys, values, out_weight.T)
    step = functools.partial(attend, place, pattern.T, queries)
    keys, values, wl = lax.optimization_barrier((keys, values, wl))
    kv = stack(keys, values)
    wl = join(wl, send(wl, xor(2)))
    kv, wl = lax.optimization_barrier((kv, wl))
    far = {level: send(kv, xor(level)) for level in (3, 5)}
    wl = join(wl, send(wl, xor(1)))
    kv, wl = lax.optimization_barrier((kv, wl))
    far[4] = send(kv, xor(4))
    wl = join(wl, send(wl, xor(0)))
    marks = pick(wl)
    kv, marks = lax.optimization_barrier((kv, marks))
    far[2] = send(kv, xor(2))
    wl = join(wl, send(marks, xor(3)))
    wl1, wl3 = send(wl, along_x(1)), send(wl, along_x(-1))
    every = mark_starts(0, 768)
    token = arrived(COST0, far[3], far[5], far[4])
    kv, token, wl = lax.optimization_barrier((kv, token, wl))
    far.update({level: send(kv, xor(level)) for level in (1, 0)})
    state = step((3, 5, 4), far, own=kv, mark=[(wl, every)], token=token, cost=COST2)
    wl1, wl3, state = lax.optimization_barrier((wl1, wl3, state))
    wl2a, wl2b = send(wl1[:HALF], along_x(1)), send(wl3[HALF:], along_x(-1))
    token = arrived(COST3, far[2])
    state = step((2,), far, state=state, mark=[(wl1, every), (wl3, every)], token=token, cost=COST)
    rest = [(wl2a, mark_starts(0, HALF)), (wl2b, mark_starts(HALF, 768))]
    late, state = lax.optimization_barrier(((far[1], far[0]), state))
    far[1], far[0] = late
    token = arrived(COST1, *late)
    pieces = (wl, wl1, wl2a, wl2b, wl3)
    pieces, token, state = lax.optimization_barrier((pieces, token, state))
    mine = step((1, 0), far, state=state, mark=rest, final=True, token=token)
    w_mine = pack(place, pieces)
    w_other = send(w_mine, lambda x, zl, y, zh, c: (x, zl, y, zh, 1 - c))
    part = project(place, mine, send(mine, to_first), send(mine, to_second), w_mine, w_other)
    total = 0.0
    for d in range(4):
        total += send(
            part[d], lambda x, zl, y, zh, c: (x, c, y, (zh + d) % NZH, zl)
        ).astype(F32)
    return total.astype(BF16)


def solution(mesh):
    in_specs = (
        P("ctx", "head"),
        P("ctx", "head"),
        P("ctx", "head"),
        P("ctx", None),
        P("head", "ctx"),
        P(),
    )
    return jax.shard_map(
        on_device, mesh=mesh, in_specs=in_specs, out_specs=P("ctx", "head"), check_vma=False
    )
```

```python
import functools

import jax
import jax.numpy as jnp
from jax import lax
from jax.experimental import pallas as pl
from jax.experimental.pallas import tpu as pltpu
from jax.sharding import PartitionSpec as P

HD = 128
BLK = 128
NX, NZL, NY, NZH, NC = 4, 2, 8, 4, 2
WROWS = 64
LROWS = 16
UNIT = WROWS + LROWS
HALF = 400
COST = 1
COST0 = 64
COST2 = 1
COST3 = 0
COST1 = 0
AXES = ("ctx", "head")
SCALE = HD**-0.5
F32 = jnp.float32
BF16 = jnp.bfloat16
VLIM = 16 << 20
HBM = pl.BlockSpec(memory_space=pltpu.HBM)
ANY = pl.BlockSpec(memory_space=pl.ANY)
SMEM = pl.BlockSpec(memory_space=pltpu.SMEM)
VMEM = pl.BlockSpec(memory_space=pltpu.VMEM)


def coords(i):
    ctx, head = divmod(i, NZH * NC)
    x, r = divmod(ctx, NZL * NY)
    zl, y = divmod(r, NY)
    zh, c = divmod(head, NC)
    return x, zl, y, zh, c


def flat(x, zl, y, zh, c):
    return ((x * NZL + zl) * NY + y) * (NZH * NC) + zh * NC + c


def send(a, to):
    pairs = [(i, flat(*to(*coords(i)))) for i in range(NX * NZL * NY * NZH * NC)]
    return lax.ppermute(a, AXES, pairs)


def xor(level):
    def to(x, zl, y, zh, c):
        ctx = ((x * NZL + zl) * NY + y) ^ (1 << level)
        x, r = divmod(ctx, NZL * NY)
        zl, y = divmod(r, NY)
        return x, zl, y, zh, c

    return to


def after(a, far, levels):
    if levels:
        a, done = lax.optimization_barrier((a, [far[l] for l in levels]))
        far.update(zip(levels, done, strict=True))
    return a


def in_hbm(a):
    return pltpu.with_memory_space_constraint(a, pltpu.HBM)


def params():
    return pltpu.CompilerParams(vmem_limit_bytes=VLIM)


def dot_nt(a, b):
    return lax.dot_general(a, b, (((1,), (1,)), ((), ())), preferred_element_type=F32)


def prepare_kernel(pool, keys, values, weight, unit, pool_v, kv_v, sem):
    copies = [
        pltpu.make_async_copy(weight, unit.at[pl.ds(0, WROWS)], sem.at[0]),
        pltpu.make_async_copy(pool, pool_v, sem.at[1]),
        pltpu.make_async_copy(keys, kv_v.at[pl.ds(0, 256)], sem.at[2]),
        pltpu.make_async_copy(values, kv_v.at[pl.ds(256, 256)], sem.at[3]),
    ]
    for copy in copies:
        copy.start()
    for copy in copies:
        copy.wait()
    pooled = [
        jnp.dot(pool_v[...], kv_v[r : r + 256, :], preferred_element_type=F32) for r in (0, 256)
    ]
    unit[WROWS:UNIT, :] = jnp.concatenate(pooled, axis=0).astype(BF16)


def prepare(pool, keys, values, weight):
    return pl.pallas_call(
        prepare_kernel,
        out_shape=jax.ShapeDtypeStruct((UNIT, 512), BF16),
        in_specs=[HBM] * 4,
        out_specs=VMEM,
        scratch_shapes=[
            pltpu.VMEM((8, 256), BF16),
            pltpu.VMEM((512, 512), BF16),
            pltpu.SemaphoreType.DMA((4,)),
        ],
        compiler_params=params(),
        name="prepare",
    )(*[in_hbm(a) for a in (pool, keys, values, weight)])


def stack_kernel(keys, values, kv, sem):
    copies = [
        pltpu.make_async_copy(keys, kv.at[pl.ds(0, 256)], sem.at[0]),
        pltpu.make_async_copy(values, kv.at[pl.ds(256, 256)], sem.at[1]),
    ]
    for copy in copies:
        copy.start()
    for copy in copies:
        copy.wait()


def stack(keys, values):
    return pl.pallas_call(
        stack_kernel,
        out_shape=jax.ShapeDtypeStruct((512, 512), BF16),
        in_specs=[HBM] * 2,
        out_specs=VMEM,
        scratch_shapes=[pltpu.SemaphoreType.DMA((2,))],
        compiler_params=params(),
        name="stack",
    )(in_hbm(keys), in_hbm(values))


def softmax_steps(states, qs, ks, vs):
    scores = [[dot_nt(q, k) * SCALE for k in row] for q, row in zip(qs, ks, strict=True)]
    tops = [
        jnp.max(functools.reduce(jnp.maximum, [p for s in row for p in tiles(s)]), axis=1, keepdims=True)
        for row in scores
    ]
    if states[0] is not None:
        tops = [jnp.maximum(t, old[0]) for t, old in zip(tops, states, strict=True)]
    weights = [[jnp.exp(s - t) for s in row] for row, t in zip(scores, tops, strict=True)]
    sums = [
        jnp.sum(sum(p for w in row for p in tiles(w)), axis=1, keepdims=True) for row in weights
    ]
    accs = [
        sum(
            jnp.dot(w.astype(BF16), v, preferred_element_type=F32)
            for w, v in zip(row, vrow, strict=True)
        )
        for row, vrow in zip(weights, vs, strict=True)
    ]
    if states[0] is not None:
        fades = [jnp.exp(old[0] - t) for old, t in zip(states, tops, strict=True)]
        sums = [s + old[1] * f for s, old, f in zip(sums, states, fades, strict=True)]
        accs = [a + old[2] * f for a, old, f in zip(accs, states, fades, strict=True)]
    return list(zip(tops, sums, accs, strict=True))


def tiles(a):
    return [a[:, i : i + 128] for i in range(0, a.shape[1], 128)]


def mark_starts(lo, hi):
    rows = [b * UNIT + WROWS for b in range(NY)] + [NY * UNIT + b * LROWS for b in range(NY)]
    return tuple(r - lo for r in rows if lo <= r < hi)


def landmarks(marks, cols):
    rows = marks[:, cols].astype(F32)
    groups = [rows[g : g + 8] for g in range(0, rows.shape[0], 8)]
    ks = jnp.concatenate(groups[0::2], axis=0)
    vs = jnp.concatenate(groups[1::2], axis=0)
    return ks.astype(BF16), vs.astype(BF16)


def attend_kernel(levels, own, carry, mark, final, token, place, pattern, q, *refs):
    refs = list(refs)
    own_ref = refs.pop(0) if own else None
    state_refs = [refs.pop(0) for _ in range(3)] if carry else None
    mark_refs = [refs.pop(0) for _ in mark]
    far = [refs.pop(0) for _ in levels]
    if token:
        refs.pop(0)
    outs = [refs.pop(0) for _ in range(1 if final else 3)]
    far_v = refs.pop(0) if levels else None
    mark_v = refs.pop(0) if mark else None
    sem = refs.pop(0)
    mark_sem = refs.pop(0) if mark else None
    copies = [pltpu.make_async_copy(r, far_v.at[i], sem.at[i]) for i, r in enumerate(far)]
    if mark:
        rows = [(r, at) for r, starts in zip(mark_refs, mark, strict=True) for at in starts]
        for i, (r, at) in enumerate(rows):
            dst = mark_v.at[pl.ds(i * LROWS, LROWS), :]
            copies.append(pltpu.make_async_copy(r.at[pl.ds(at, LROWS), :], dst, mark_sem.at[i]))
    for copy in copies:
        copy.start()
    for copy in copies:
        copy.wait()
    streams = 4 if final else 2
    for pair in range(0, 4, streams):
        spots, states, qs, kss, vss = [], [], [], [], []
        for h in range(pair, pair + streams):
            cols = slice(h * HD, (h + 1) * HD)
            marks = landmarks(mark_v, cols) if mark else None
            for j in range(2):
                rows = slice(j * BLK, (j + 1) * BLK)
                ks, vs = [], []
                if own:
                    ks.append(own_ref[0:256, cols])
                    vs.append(own_ref[256:512, cols])
                if mark:
                    ks.append(marks[0])
                    vs.append(marks[1])
                for i, level in enumerate(levels):
                    at = pl.multiple_of((pattern[1 + level, place[2] + j] & 1) * BLK, BLK)
                    ks.append(far_v[i, pl.ds(at, BLK), cols])
                    vs.append(far_v[i, pl.ds(256 + at, BLK), cols])
                state = None
                if carry:
                    top, total, acc = state_refs
                    first = slice(h * HD, h * HD + 1)
                    state = (top[rows, first], total[rows, first], acc[rows, cols])
                spots.append((rows, cols))
                states.append(state)
                qs.append(q[rows, cols])
                kss.append(ks)
                vss.append(vs)
        for (rows, cols), (m, s, a) in zip(
            spots, softmax_steps(states, qs, kss, vss), strict=True
        ):
            if final:
                outs[0][rows, cols] = (a / s).astype(BF16)
            else:
                outs[0][rows, cols] = jnp.broadcast_to(m, (BLK, HD))
                outs[1][rows, cols] = jnp.broadcast_to(s, (BLK, HD))
                outs[2][rows, cols] = a


def attend(place, pattern, q, levels, far, own=None, state=None, mark=(), final=False, cost=1, token=None):
    args, specs = [place, pattern, q], [SMEM, SMEM, VMEM]
    if own is not None:
        args, specs = [*args, own], [*specs, VMEM]
    if state is not None:
        args, specs = [*args, *state], specs + [VMEM] * 3
    args += [a for a, _ in mark]
    specs += [ANY] * len(mark)
    args += [in_hbm(far[l]) for l in levels]
    specs += [HBM] * len(levels)
    if token is not None:
        args, specs = [*args, token], [*specs, ANY]
    scratch = [pltpu.VMEM((len(levels), 512, 512), BF16)] if levels else []
    groups = sum(len(starts) for _, starts in mark)
    if mark:
        scratch.append(pltpu.VMEM((groups * LROWS, 512), BF16))
    scratch.append(pltpu.SemaphoreType.DMA((len(levels) + 1,)))
    if mark:
        scratch.append(pltpu.SemaphoreType.DMA((groups,)))
    count = 128 * len(levels) + 256 * (own is not None) + 8 * groups
    return pl.pallas_call(
        functools.partial(
            attend_kernel,
            levels,
            own is not None,
            state is not None,
            tuple(starts for _, starts in mark),
            final,
            token is not None,
        ),
        out_shape=jax.ShapeDtypeStruct((256, 512), BF16)
        if final
        else (jax.ShapeDtypeStruct((256, 512), F32),) * 3,
        in_specs=specs,
        out_specs=VMEM if final else (VMEM,) * 3,
        scratch_shapes=scratch,
        compiler_params=params(),
        name="attend",
        cost_estimate=pl.CostEstimate(
            flops=cost * 4 * 256 * 512 * count,
            bytes_accessed=4 << 20,
            transcendentals=1024 * count,
        ),
    )(*args)


def pack_kernel(place, w0, w1, w2a, w2b, w3, out):
    y = place[3]
    chunks = (((w0, 0, 768),), ((w1, 0, 768),), ((w2a, 0, HALF), (w2b, HALF, 768)))
    chunks += (((w3, 0, 768),),)
    for i, pieces in enumerate(chunks):
        for p in range(NY):
            at = pl.multiple_of((y ^ (4 * (p & 1) + (p & 2) + (p >> 2))) * WROWS, WROWS)
            [(ref, lo)] = [(r, lo) for r, lo, hi in pieces if lo <= p * UNIT < hi]
            out[i, pl.ds(at, WROWS), :] = ref[p * UNIT - lo : p * UNIT - lo + WROWS, :]


def pack(place, wl):
    return pl.pallas_call(
        pack_kernel,
        out_shape=jax.ShapeDtypeStruct((NX, NY * WROWS, 512), BF16),
        in_specs=[SMEM] + [VMEM] * 5,
        out_specs=VMEM,
        compiler_params=params(),
        name="pack",
    )(place, *wl)


def project_kernel(place, mine, got1, got2, w_mine, w_other, *outs):
    step, same = place[0], place[1] == 1
    a, b = mine[...], got1[...]
    first = jnp.where(same, a, b)
    second = jnp.where(same, b, got2[...])
    for d in range(4):
        shift = (step - d) & 3
        outs[d][...] = (dot_nt(first, w_mine[shift]) + dot_nt(second, w_other[shift])).astype(BF16)


def project(place, mine, got1, got2, w_mine, w_other):
    return pl.pallas_call(
        project_kernel,
        out_shape=(jax.ShapeDtypeStruct((256, 512), BF16),) * 4,
        in_specs=[SMEM] + [VMEM] * 5,
        out_specs=(VMEM,) * 4,
        compiler_params=params(),
        name="project",
        cost_estimate=pl.CostEstimate(
            flops=2 * 512 * 512 * 2048, bytes_accessed=6 << 20, transcendentals=0
        ),
    )(place, mine, got1, got2, w_mine, w_other)


def join_kernel(a, b, out):
    n = a.shape[0]
    out[0:n, :] = a[...]
    out[n:, :] = b[...]


def join(a, b):
    return pl.pallas_call(
        join_kernel,
        out_shape=jax.ShapeDtypeStruct((a.shape[0] + b.shape[0], 512), BF16),
        in_specs=[VMEM] * 2,
        out_specs=VMEM,
        compiler_params=params(),
        name="join",
    )(a, b)


def arrived_kernel(*refs):
    refs[-1][...] = jnp.zeros_like(refs[-1])


def arrived(cost, *arrays):
    return pl.pallas_call(
        arrived_kernel,
        out_shape=jax.ShapeDtypeStruct((8, 128), F32),
        in_specs=[HBM] * len(arrays),
        out_specs=VMEM,
        compiler_params=params(),
        name="arrived",
        cost_estimate=pl.CostEstimate(flops=cost << 27, bytes_accessed=4 << 20, transcendentals=0),
    )(*[in_hbm(a) for a in arrays])


def pick_kernel(a, out):
    for p in range(NY):
        out[p * LROWS : (p + 1) * LROWS, :] = a[p * UNIT + WROWS : (p + 1) * UNIT, :]


def pick(a):
    return pl.pallas_call(
        pick_kernel,
        out_shape=jax.ShapeDtypeStruct((NY * LROWS, 512), BF16),
        in_specs=[VMEM],
        out_specs=VMEM,
        compiler_params=params(),
        name="pick",
    )(a)


def along_x(k):
    return lambda x, zl, y, zh, c: ((x + k) % NX, zl, y, zh, c)


def to_first(x, zl, y, zh, c):
    return (x, zl, y, zh, 1 - c) if zl != c else (x, 1 - zl, y, zh, c)


def to_second(x, zl, y, zh, c):
    return (x, 1 - zl, y, zh, 1 - c) if zl != c else (x, zl, y, zh, c)


def on_device(queries, keys, values, pool_weight, out_weight, pattern):
    ctx, head = lax.axis_index("ctx"), lax.axis_index("head")
    same = (((ctx >> 3) ^ head) & 1) ^ 1
    place = jnp.stack([(ctx >> 4) + NX - (head >> 1), same, ctx * 2, ctx & 7])

    wl = prepare(pool_weight, keys, values, out_weight.T)
    step = functools.partial(attend, place, pattern.T, queries)
    keys, values, wl = lax.optimization_barrier((keys, values, wl))
    kv = stack(keys, values)
    wl = join(wl, send(wl, xor(2)))
    kv, wl = lax.optimization_barrier((kv, wl))
    far = {level: send(kv, xor(level)) for level in (3, 5)}
    wl = join(wl, send(wl, xor(1)))
    kv, wl = lax.optimization_barrier((kv, wl))
    far[4] = send(kv, xor(4))
    wl = join(wl, send(wl, xor(0)))
    marks = pick(wl)
    kv, marks = lax.optimization_barrier((kv, marks))
    far[2] = send(kv, xor(2))
    wl = join(wl, send(marks, xor(3)))
    wl1, wl3 = send(wl, along_x(1)), send(wl, along_x(-1))
    every = mark_starts(0, 768)
    token = arrived(COST0, far[3], far[5], far[4])
    kv, token, wl = lax.optimization_barrier((kv, token, wl))
    far.update({level: send(kv, xor(level)) for level in (1, 0)})
    state = step((3, 5, 4), far, own=kv, mark=[(wl, every)], token=token, cost=COST2)
    wl1, wl3, state = lax.optimization_barrier((wl1, wl3, state))
    wl2a, wl2b = send(wl1[:HALF], along_x(1)), send(wl3[HALF:], along_x(-1))
    token = arrived(COST3, far[2])
    state = step((2,), far, state=state, mark=[(wl1, every), (wl3, every)], token=token, cost=COST)
    rest = [(wl2a, mark_starts(0, HALF)), (wl2b, mark_starts(HALF, 768))]
    pieces = (wl, wl1, wl2a, wl2b, wl3)
    pieces, state = lax.optimization_barrier((pieces, state))
    w_mine = pack(place, pieces)
    late, w_mine = lax.optimization_barrier(((far[1], far[0]), w_mine))
    far[1], far[0] = late
    token = arrived(COST1, *late)
    mine = step((1, 0), far, state=state, mark=rest, final=True, token=token)
    w_other = send(w_mine, lambda x, zl, y, zh, c: (x, zl, y, zh, 1 - c))
    part = project(place, mine, send(mine, to_first), send(mine, to_second), w_mine, w_other)
    total = 0.0
    for d in (2, 1, 3, 0):
        total += send(
            part[d], lambda x, zl, y, zh, c: (x, c, y, (zh + d) % NZH, zl)
        ).astype(F32)
    return total.astype(BF16)


def solution(mesh):
    in_specs = (
        P("ctx", "head"),
        P("ctx", "head"),
        P("ctx", "head"),
        P("ctx", None),
        P("head", "ctx"),
        P(),
    )
    return jax.shard_map(
        on_device, mesh=mesh, in_specs=in_specs, out_specs=P("ctx", "head"), check_vma=False
    )
```

```python
import functools

import jax
import jax.numpy as jnp
from jax import lax
from jax.experimental import pallas as pl
from jax.experimental.pallas import tpu as pltpu
from jax.sharding import PartitionSpec as P

HD = 128
BLK = 128
NX, NZL, NY, NZH, NC = 4, 2, 8, 4, 2
WROWS = 64
LROWS = 16
UNIT = WROWS + LROWS
HALF = 400
COST = 1
COST0 = 64
COST2 = 1
COST3 = 0
COST1 = 0
AXES = ("ctx", "head")
SCALE = HD**-0.5
F32 = jnp.float32
BF16 = jnp.bfloat16
VLIM = 16 << 20
HBM = pl.BlockSpec(memory_space=pltpu.HBM)
ANY = pl.BlockSpec(memory_space=pl.ANY)
SMEM = pl.BlockSpec(memory_space=pltpu.SMEM)
VMEM = pl.BlockSpec(memory_space=pltpu.VMEM)


def coords(i):
    ctx, head = divmod(i, NZH * NC)
    x, r = divmod(ctx, NZL * NY)
    zl, y = divmod(r, NY)
    zh, c = divmod(head, NC)
    return x, zl, y, zh, c


def flat(x, zl, y, zh, c):
    return ((x * NZL + zl) * NY + y) * (NZH * NC) + zh * NC + c


def send(a, to):
    pairs = [(i, flat(*to(*coords(i)))) for i in range(NX * NZL * NY * NZH * NC)]
    return lax.ppermute(a, AXES, pairs)


def xor(level):
    def to(x, zl, y, zh, c):
        ctx = ((x * NZL + zl) * NY + y) ^ (1 << level)
        x, r = divmod(ctx, NZL * NY)
        zl, y = divmod(r, NY)
        return x, zl, y, zh, c

    return to


def after(a, far, levels):
    if levels:
        a, done = lax.optimization_barrier((a, [far[l] for l in levels]))
        far.update(zip(levels, done, strict=True))
    return a


def in_hbm(a):
    return pltpu.with_memory_space_constraint(a, pltpu.HBM)


def params():
    return pltpu.CompilerParams(vmem_limit_bytes=VLIM)


def dot_nt(a, b):
    return lax.dot_general(a, b, (((1,), (1,)), ((), ())), preferred_element_type=F32)


def prepare_kernel(pool, keys, values, weight, unit, pool_v, kv_v, sem):
    copies = [
        pltpu.make_async_copy(weight, unit.at[pl.ds(0, WROWS)], sem.at[0]),
        pltpu.make_async_copy(pool, pool_v, sem.at[1]),
        pltpu.make_async_copy(keys, kv_v.at[pl.ds(0, 256)], sem.at[2]),
        pltpu.make_async_copy(values, kv_v.at[pl.ds(256, 256)], sem.at[3]),
    ]
    for copy in copies:
        copy.start()
    for copy in copies:
        copy.wait()
    pooled = [
        jnp.dot(pool_v[...], kv_v[r : r + 256, :], preferred_element_type=F32) for r in (0, 256)
    ]
    unit[WROWS:UNIT, :] = jnp.concatenate(pooled, axis=0).astype(BF16)


def prepare(pool, keys, values, weight):
    return pl.pallas_call(
        prepare_kernel,
        out_shape=jax.ShapeDtypeStruct((UNIT, 512), BF16),
        in_specs=[HBM] * 4,
        out_specs=VMEM,
        scratch_shapes=[
            pltpu.VMEM((8, 256), BF16),
            pltpu.VMEM((512, 512), BF16),
            pltpu.SemaphoreType.DMA((4,)),
        ],
        compiler_params=params(),
        name="prepare",
    )(*[in_hbm(a) for a in (pool, keys, values, weight)])


def stack_kernel(keys, values, kv, sem):
    copies = [
        pltpu.make_async_copy(keys, kv.at[pl.ds(0, 256)], sem.at[0]),
        pltpu.make_async_copy(values, kv.at[pl.ds(256, 256)], sem.at[1]),
    ]
    for copy in copies:
        copy.start()
    for copy in copies:
        copy.wait()


def stack(keys, values):
    return pl.pallas_call(
        stack_kernel,
        out_shape=jax.ShapeDtypeStruct((512, 512), BF16),
        in_specs=[HBM] * 2,
        out_specs=VMEM,
        scratch_shapes=[pltpu.SemaphoreType.DMA((2,))],
        compiler_params=params(),
        name="stack",
    )(in_hbm(keys), in_hbm(values))


def softmax_steps(states, qs, ks, vs):
    scores = [[dot_nt(q, k) * SCALE for k in row] for q, row in zip(qs, ks, strict=True)]
    tops = [
        jnp.max(functools.reduce(jnp.maximum, [p for s in row for p in tiles(s)]), axis=1, keepdims=True)
        for row in scores
    ]
    if states[0] is not None:
        tops = [jnp.maximum(t, old[0]) for t, old in zip(tops, states, strict=True)]
    weights = [[jnp.exp(s - t) for s in row] for row, t in zip(scores, tops, strict=True)]
    sums = [
        jnp.sum(sum(p for w in row for p in tiles(w)), axis=1, keepdims=True) for row in weights
    ]
    accs = [
        sum(
            jnp.dot(w.astype(BF16), v, preferred_element_type=F32)
            for w, v in zip(row, vrow, strict=True)
        )
        for row, vrow in zip(weights, vs, strict=True)
    ]
    if states[0] is not None:
        fades = [jnp.exp(old[0] - t) for old, t in zip(states, tops, strict=True)]
        sums = [s + old[1] * f for s, old, f in zip(sums, states, fades, strict=True)]
        accs = [a + old[2] * f for a, old, f in zip(accs, states, fades, strict=True)]
    return list(zip(tops, sums, accs, strict=True))


def tiles(a):
    return [a[:, i : i + 128] for i in range(0, a.shape[1], 128)]


def mark_starts(lo, hi):
    rows = [b * UNIT + WROWS for b in range(NY)] + [NY * UNIT + b * LROWS for b in range(NY)]
    return tuple(r - lo for r in rows if lo <= r < hi)


def landmarks(marks, cols):
    rows = marks[:, cols].astype(F32)
    groups = [rows[g : g + 8] for g in range(0, rows.shape[0], 8)]
    ks = jnp.concatenate(groups[0::2], axis=0)
    vs = jnp.concatenate(groups[1::2], axis=0)
    return ks.astype(BF16), vs.astype(BF16)


def attend_kernel(levels, own, carry, mark, final, token, place, pattern, q, *refs):
    refs = list(refs)
    own_ref = refs.pop(0) if own else None
    state_refs = [refs.pop(0) for _ in range(3)] if carry else None
    mark_refs = [refs.pop(0) for _ in mark]
    far = [refs.pop(0) for _ in levels]
    if token:
        refs.pop(0)
    outs = [refs.pop(0) for _ in range(1 if final else 3)]
    far_v = refs.pop(0) if levels else None
    mark_v = refs.pop(0) if mark else None
    sem = refs.pop(0)
    mark_sem = refs.pop(0) if mark else None
    copies = [pltpu.make_async_copy(r, far_v.at[i], sem.at[i]) for i, r in enumerate(far)]
    if mark:
        rows = [(r, at) for r, starts in zip(mark_refs, mark, strict=True) for at in starts]
        for i, (r, at) in enumerate(rows):
            dst = mark_v.at[pl.ds(i * LROWS, LROWS), :]
            copies.append(pltpu.make_async_copy(r.at[pl.ds(at, LROWS), :], dst, mark_sem.at[i]))
    for copy in copies:
        copy.start()
    for copy in copies:
        copy.wait()
    streams = 4 if final else 2
    for pair in range(0, 4, streams):
        spots, states, qs, kss, vss = [], [], [], [], []
        for h in range(pair, pair + streams):
            cols = slice(h * HD, (h + 1) * HD)
            marks = landmarks(mark_v, cols) if mark else None
            for j in range(2):
                rows = slice(j * BLK, (j + 1) * BLK)
                ks, vs = [], []
                if own:
                    ks.append(own_ref[0:256, cols])
                    vs.append(own_ref[256:512, cols])
                if mark:
                    ks.append(marks[0])
                    vs.append(marks[1])
                for i, level in enumerate(levels):
                    at = pl.multiple_of((pattern[1 + level, place[2] + j] & 1) * BLK, BLK)
                    ks.append(far_v[i, pl.ds(at, BLK), cols])
                    vs.append(far_v[i, pl.ds(256 + at, BLK), cols])
                state = None
                if carry:
                    top, total, acc = state_refs
                    first = slice(h * HD, h * HD + 1)
                    state = (top[rows, first], total[rows, first], acc[rows, cols])
                spots.append((rows, cols))
                states.append(state)
                qs.append(q[rows, cols])
                kss.append(ks)
                vss.append(vs)
        for (rows, cols), (m, s, a) in zip(
            spots, softmax_steps(states, qs, kss, vss), strict=True
        ):
            if final:
                outs[0][rows, cols] = (a / s).astype(BF16)
            else:
                outs[0][rows, cols] = jnp.broadcast_to(m, (BLK, HD))
                outs[1][rows, cols] = jnp.broadcast_to(s, (BLK, HD))
                outs[2][rows, cols] = a


def attend(place, pattern, q, levels, far, own=None, state=None, mark=(), final=False, cost=1, token=None):
    args, specs = [place, pattern, q], [SMEM, SMEM, VMEM]
    if own is not None:
        args, specs = [*args, own], [*specs, VMEM]
    if state is not None:
        args, specs = [*args, *state], specs + [VMEM] * 3
    args += [a for a, _ in mark]
    specs += [ANY] * len(mark)
    args += [far[l] if final else in_hbm(far[l]) for l in levels]
    specs += [ANY if final else HBM] * len(levels)
    if token is not None:
        args, specs = [*args, token], [*specs, ANY]
    scratch = [pltpu.VMEM((len(levels), 512, 512), BF16)] if levels else []
    groups = sum(len(starts) for _, starts in mark)
    if mark:
        scratch.append(pltpu.VMEM((groups * LROWS, 512), BF16))
    scratch.append(pltpu.SemaphoreType.DMA((len(levels) + 1,)))
    if mark:
        scratch.append(pltpu.SemaphoreType.DMA((groups,)))
    count = 128 * len(levels) + 256 * (own is not None) + 8 * groups
    return pl.pallas_call(
        functools.partial(
            attend_kernel,
            levels,
            own is not None,
            state is not None,
            tuple(starts for _, starts in mark),
            final,
            token is not None,
        ),
        out_shape=jax.ShapeDtypeStruct((256, 512), BF16)
        if final
        else (jax.ShapeDtypeStruct((256, 512), F32),) * 3,
        in_specs=specs,
        out_specs=VMEM if final else (VMEM,) * 3,
        scratch_shapes=scratch,
        compiler_params=params(),
        name="attend",
        cost_estimate=pl.CostEstimate(
            flops=cost * 4 * 256 * 512 * count,
            bytes_accessed=4 << 20,
            transcendentals=1024 * count,
        ),
    )(*args)


def pack_kernel(place, w0, w1, w2a, w2b, w3, out):
    y = place[3]
    chunks = (((w0, 0, 768),), ((w1, 0, 768),), ((w2a, 0, HALF), (w2b, HALF, 768)))
    chunks += (((w3, 0, 768),),)
    for i, pieces in enumerate(chunks):
        for p in range(NY):
            at = pl.multiple_of((y ^ (4 * (p & 1) + (p & 2) + (p >> 2))) * WROWS, WROWS)
            [(ref, lo)] = [(r, lo) for r, lo, hi in pieces if lo <= p * UNIT < hi]
            out[i, pl.ds(at, WROWS), :] = ref[p * UNIT - lo : p * UNIT - lo + WROWS, :]


def pack(place, wl):
    return pl.pallas_call(
        pack_kernel,
        out_shape=jax.ShapeDtypeStruct((NX, NY * WROWS, 512), BF16),
        in_specs=[SMEM] + [VMEM] * 5,
        out_specs=VMEM,
        compiler_params=params(),
        name="pack",
    )(place, *wl)


def project_kernel(place, mine, got1, got2, w_mine, w_other, *outs):
    step, same = place[0], place[1] == 1
    a, b = mine[...], got1[...]
    first = jnp.where(same, a, b)
    second = jnp.where(same, b, got2[...])
    for d in range(4):
        shift = (step - d) & 3
        outs[d][...] = (dot_nt(first, w_mine[shift]) + dot_nt(second, w_other[shift])).astype(BF16)


def project(place, mine, got1, got2, w_mine, w_other):
    return pl.pallas_call(
        project_kernel,
        out_shape=(jax.ShapeDtypeStruct((256, 512), BF16),) * 4,
        in_specs=[SMEM] + [VMEM] * 5,
        out_specs=(VMEM,) * 4,
        compiler_params=params(),
        name="project",
        cost_estimate=pl.CostEstimate(
            flops=2 * 512 * 512 * 2048, bytes_accessed=6 << 20, transcendentals=0
        ),
    )(place, mine, got1, got2, w_mine, w_other)


def join_kernel(a, b, out):
    n = a.shape[0]
    out[0:n, :] = a[...]
    out[n:, :] = b[...]


def join(a, b):
    return pl.pallas_call(
        join_kernel,
        out_shape=jax.ShapeDtypeStruct((a.shape[0] + b.shape[0], 512), BF16),
        in_specs=[VMEM] * 2,
        out_specs=VMEM,
        compiler_params=params(),
        name="join",
    )(a, b)


def arrived_kernel(*refs):
    refs[-1][...] = jnp.zeros_like(refs[-1])


def arrived(cost, *arrays):
    return pl.pallas_call(
        arrived_kernel,
        out_shape=jax.ShapeDtypeStruct((8, 128), F32),
        in_specs=[ANY] * len(arrays),
        out_specs=VMEM,
        compiler_params=params(),
        name="arrived",
        cost_estimate=pl.CostEstimate(flops=cost << 27, bytes_accessed=4 << 20, transcendentals=0),
    )(*arrays)


def pick_kernel(a, out):
    for p in range(NY):
        out[p * LROWS : (p + 1) * LROWS, :] = a[p * UNIT + WROWS : (p + 1) * UNIT, :]


def pick(a):
    return pl.pallas_call(
        pick_kernel,
        out_shape=jax.ShapeDtypeStruct((NY * LROWS, 512), BF16),
        in_specs=[VMEM],
        out_specs=VMEM,
        compiler_params=params(),
        name="pick",
    )(a)


def along_x(k):
    return lambda x, zl, y, zh, c: ((x + k) % NX, zl, y, zh, c)


def to_first(x, zl, y, zh, c):
    return (x, zl, y, zh, 1 - c) if zl != c else (x, 1 - zl, y, zh, c)


def to_second(x, zl, y, zh, c):
    return (x, 1 - zl, y, zh, 1 - c) if zl != c else (x, zl, y, zh, c)


def on_device(queries, keys, values, pool_weight, out_weight, pattern):
    ctx, head = lax.axis_index("ctx"), lax.axis_index("head")
    same = (((ctx >> 3) ^ head) & 1) ^ 1
    place = jnp.stack([(ctx >> 4) + NX - (head >> 1), same, ctx * 2, ctx & 7])

    wl = prepare(pool_weight, keys, values, out_weight.T)
    step = functools.partial(attend, place, pattern.T, queries)
    keys, values, wl = lax.optimization_barrier((keys, values, wl))
    kv = stack(keys, values)
    wl = join(wl, send(wl, xor(2)))
    kv, wl = lax.optimization_barrier((kv, wl))
    far = {level: send(kv, xor(level)) for level in (3, 5)}
    wl = join(wl, send(wl, xor(1)))
    kv, wl = lax.optimization_barrier((kv, wl))
    far[4] = send(kv, xor(4))
    wl = join(wl, send(wl, xor(0)))
    marks = pick(wl)
    kv, marks = lax.optimization_barrier((kv, marks))
    far[2] = send(kv, xor(2))
    wl = join(wl, send(marks, xor(3)))
    wl1, wl3 = send(wl, along_x(1)), send(wl, along_x(-1))
    every = mark_starts(0, 768)
    token = arrived(COST0, far[3], far[5], far[4])
    kv, token, wl = lax.optimization_barrier((kv, token, wl))
    far.update({level: send(kv, xor(level)) for level in (1, 0)})
    state = step((3, 5, 4), far, own=kv, mark=[(wl, every)], token=token, cost=COST2)
    wl1, wl3, state = lax.optimization_barrier((wl1, wl3, state))
    wl2a, wl2b = send(wl1[:HALF], along_x(1)), send(wl3[HALF:], along_x(-1))
    token = arrived(COST3, far[2])
    state = step((2,), far, state=state, mark=[(wl1, every), (wl3, every)], token=token, cost=COST)
    rest = [(wl2a, mark_starts(0, HALF)), (wl2b, mark_starts(HALF, 768))]
    pieces = (wl, wl1, wl2a, wl2b, wl3)
    pieces, state = lax.optimization_barrier((pieces, state))
    w_mine = pack(place, pieces)
    late, w_mine = lax.optimization_barrier(((far[1], far[0]), w_mine))
    far[1], far[0] = late
    token = arrived(COST1, *late)
    mine = step((1, 0), far, state=state, mark=rest, final=True, token=token)
    w_other = send(w_mine, lambda x, zl, y, zh, c: (x, zl, y, zh, 1 - c))
    part = project(place, mine, send(mine, to_first), send(mine, to_second), w_mine, w_other)
    total = 0.0
    for d in (2, 1, 3, 0):
        total += send(
            part[d], lambda x, zl, y, zh, c: (x, c, y, (zh + d) % NZH, zl)
        ).astype(F32)
    return total.astype(BF16)


def solution(mesh):
    in_specs = (
        P("ctx", "head"),
        P("ctx", "head"),
        P("ctx", "head"),
        P("ctx", None),
        P("head", "ctx"),
        P(),
    )
    return jax.shard_map(
        on_device, mesh=mesh, in_specs=in_specs, out_specs=P("ctx", "head"), check_vma=False
    )
```
